32 devices in a mesh: group: 2 (over x), ctx: 8 (over z, y), tp: 2 (over core).
Axes of the slice: x: 2, y: 2, z: 4, core: 2. Of those that a mesh axis runs over, the one named last changes fastest.
Arguments:
- x_in: bfloat16 [4096, 4096], P(('group', 'ctx', 'tp')), parts along dimension 0, may hold values from -6 to 6
- b_in: bfloat16 [4096, 512], P(('group', 'ctx', 'tp')), parts along dimension 0, may hold values from -6 to 6
- c_in: bfloat16 [4096, 512], P(('group', 'ctx', 'tp')), parts along dimension 0, may hold values from -6 to 6
- z_in: bfloat16 [4096, 4096], P(('group', 'ctx', 'tp')), parts along dimension 0, may hold values from -6 to 6
- dt_raw: bfloat16 [4096, 64], P(('group', 'ctx', 'tp')), parts along dimension 0, may hold values from -3 to 3
- conv_x: float32 [4, 4096], replicated, may hold values from -3 to 3
- conv_b: float32 [4, 512], replicated, may hold values from -3 to 3
- conv_c: float32 [4, 512], replicated, may hold values from -3 to 3
- decay_rate: float32 [64], replicated, may hold values from 3e-05 to 0.06
- dt_bias: float32 [64], replicated, may hold values from -1.5 to -0.5
- skip_scale: float32 [64], replicated, may hold values from 0.5 to 1.5
- norm_gain: float32 [4096], replicated, may hold values from 0.1 to 1.9
- w_value: float32 [4096], replicated, may hold values from -0.4 to 0.4
- resets: int32 [4096], P(('group', 'ctx')), parts along dimension 0, may hold values 0 or 1
- bucket: int32 [4096], P(('group', 'ctx')), parts along dimension 0, may hold values from 0 to 255
- return_table: float32 [256], replicated, may hold values from -16 to 16
Outputs:
- values: float32 [4096], P(('group', 'ctx', 'tp')), parts along dimension 0
- grad_x: bfloat16 [4096, 4096], P(('group', 'ctx', 'tp')), parts along dimension 0
- grad_b: bfloat16 [4096, 512], P(('group', 'ctx', 'tp')), parts along dimension 0
- grad_c: bfloat16 [4096, 512], P(('group', 'ctx', 'tp')), parts along dimension 0
- grad_z: bfloat16 [4096, 4096], P(('group', 'ctx', 'tp')), parts along dimension 0
- grad_dt: bfloat16 [4096, 64], P(('group', 'ctx', 'tp')), parts along dimension 0
The draws below stay inside these ranges and needn't reach their ends.
There are 2 independent parts, one for each index of `group`. The reference program is written for one: setup_inputs(seed, part) draws one part's arguments, and reference() takes and returns one part's arrays. A program takes and returns all parts, laid end to end along the dimension named above; an argument that names none is the same for every part. Nothing has to cross between parts.
All inputs are finite; a program needn't handle non-finite values. No bound on the sum of `resets` on one device may be relied on, other than what follows from the above.
Results may differ from the reference program's by a relative error of at most 0.0058.
Values may be sent and summed in bfloat16 or wider, within the bound.
A program may use at most 192 MiB of HBM per device.

```python
import math
from functools import partial
import jax
import jax.numpy as jnp
from jax import lax

HEADS = 64
HEAD_DIM = 64
STATE = 128
GROUPS = 4
BLOCK = 128
BUCKETS = 256
SEQ = 2048
CH = 4096


def set_ends(result, rng, low, top_value):
    longest = result.shape.index(max(result.shape))
    spots = []
    for shift in (0, 1):
        where = [jax.random.randint(jax.random.fold_in(rng, axis), (), 0, length) for axis, length in enumerate(result.shape)]
        where[longest] = (where[longest] + shift) % result.shape[longest]
        spots.append(tuple(where))
    return result.at[spots[0]].set(low).at[spots[1]].set(top_value)


def block_levels(key, shape, cuts, low, top_value):
    def one(dim, parts):
        draws = jax.random.uniform(jax.random.fold_in(jax.random.fold_in(key, 6), dim), (parts,), jnp.float32, low / len(cuts), top_value / len(cuts))
        return jnp.repeat(jnp.exp(draws), shape[dim] // parts).reshape((-1,) + (1,) * (len(shape) - dim - 1))

    loudness = one(*cuts[0])
    for cut in cuts[1:]:
        loudness = loudness * one(*cut)
    return loudness


def centred(stream_key, extent, deviation, limit, split=(), kind=jnp.bfloat16):
    values = jax.random.normal(stream_key, extent, jnp.float32) * deviation
    if len(split) > 0:
        values = block_levels(stream_key, extent, split, -0.22, 0.18) * values
    return jnp.clip(values, min=-limit, max=limit).astype(kind)


def setup_inputs(seed: int = 0, part: int = 0) -> dict:
    key_list = jax.random.split(jax.random.key(seed), 17)
    part_keys = jax.random.split(jax.random.fold_in(key_list[16], part), 17)
    x_in = centred(part_keys[0], (SEQ, CH), 1.0, 6.0, ((0, 16),))
    b_in = centred(part_keys[1], (SEQ, GROUPS * STATE), 1.0, 6.0, ((0, 16),))
    c_in = centred(part_keys[2], (SEQ, GROUPS * STATE), 1.0, 6.0, ((0, 16),))
    z_in = centred(part_keys[3], (SEQ, CH), 1.0, 6.0, ((0, 16),))
    dt_raw = centred(part_keys[4], (SEQ, HEADS), 0.6, 3.0, ((0, 16),))
    conv_x = centred(key_list[5], (4, CH), 0.5, 3.0, (), jnp.float32)
    conv_b = centred(key_list[6], (4, GROUPS * STATE), 0.5, 3.0, (), jnp.float32)
    conv_c = centred(key_list[7], (4, GROUPS * STATE), 0.5, 3.0, (), jnp.float32)
    decay_rate = jnp.clip(jnp.exp(jax.random.uniform(key_list[8], (HEADS,), jnp.float32, math.log(2.9999999242136255e-05), math.log(0.06))), 2.9999999242136255e-05, 0.06)
    dt_bias = jnp.clip(jax.random.uniform(key_list[9], (HEADS,), jnp.float32, -1.5, -0.5), -1.5, -0.5)
    skip_scale = jnp.clip(jax.random.uniform(key_list[10], (HEADS,), jnp.float32, 0.5, 1.5), 0.5, 1.5)
    norm_gain = jnp.clip(1.0 + 0.18 * jax.random.normal(key_list[11], (CH,), jnp.float32), 0.1, 1.9)
    w_value = centred(key_list[12], (CH,), 0.0625, 0.4, (), jnp.float32)
    resets = set_ends((jax.random.randint(part_keys[13], (SEQ,), 0, 2048) < 1).astype(jnp.int32), jax.random.fold_in(part_keys[13], 1), 0, 1)
    bucket = set_ends(jax.random.randint(part_keys[14], (SEQ,), 0, BUCKETS), jax.random.fold_in(part_keys[14], 1), 0, BUCKETS - 1).astype(jnp.int32)
    return_table = centred(key_list[15], (BUCKETS,), 4.0, 16.0, (), jnp.float32)
    return dict(x_in=x_in, b_in=b_in, c_in=c_in, z_in=z_in, dt_raw=dt_raw, conv_x=conv_x, conv_b=conv_b, conv_c=conv_c, decay_rate=decay_rate, dt_bias=dt_bias, skip_scale=skip_scale, norm_gain=norm_gain, w_value=w_value, resets=resets, bucket=bucket, return_table=return_table)


epsilon = 1e-05
highest = lax.Precision.HIGHEST

def round_keep(value):
    narrow = lax.optimization_barrier(value.astype(jnp.bfloat16))
    return value + lax.stop_gradient(narrow.astype(jnp.float32) - value)

def shift_rows(values, amount):
    filler = jnp.zeros((amount,) + values.shape[1:], values.dtype)
    return jnp.concatenate([filler, values[:values.shape[0] - amount]], axis=0)

def seen_resets(reset_real):
    first = reset_real
    second = jnp.maximum(first, shift_rows(reset_real, 1))
    third = jnp.maximum(second, shift_rows(reset_real, 2))
    return (first, second, third)

def conv_silu(extended, weight, seen_flags):
    row_count = extended.shape[0] - 3
    summed = weight[0][None, :] * extended[3:]
    for offset in range(1, 4):
        valid = 1.0 - seen_flags[offset - 1]
        summed = summed + weight[offset][None, :] * extended[3 - offset:3 - offset + row_count] * valid[:, None]
    return round_keep(jax.nn.silu(summed))

def block_decays(dt_rows, decay_rate, reset_real):
    cumulative = jnp.cumsum(-dt_rows * decay_rate[None, :], axis=0)
    counts = jnp.cumsum(reset_real, axis=0)
    return (cumulative, counts)

def block_state(x_conv, b_conv, dt_rows, cumulative, counts, per_group):
    row_count, head_count = dt_rows.shape
    alive = jnp.where(counts == counts[-1], 1.0, 0.0)
    weight_end = jnp.exp(cumulative[-1][None, :] - cumulative) * alive[:, None] * dt_rows
    x_heads = x_conv.reshape(row_count, head_count, -1) * weight_end[:, :, None]
    b_heads = jnp.repeat(b_conv.reshape(row_count, head_count // per_group, -1), per_group, axis=1)
    state_add = jnp.einsum('shp,shn->hpn', x_heads, b_heads, precision=highest)
    block_decay = jnp.exp(cumulative[-1]) * jnp.where(counts[-1] == 0.0, 1.0, 0.0)
    return (state_add, block_decay)

def block_output(x_conv, b_conv, c_conv, dt_rows, cumulative, counts, start_state, per_group):
    row_count, head_count = dt_rows.shape
    group_count = head_count // per_group
    b_groups = b_conv.reshape(row_count, group_count, -1)
    c_groups = c_conv.reshape(row_count, group_count, -1)
    scores = jnp.einsum('tgn,sgn->gts', c_groups, b_groups, precision=highest)
    rows_iota = lax.broadcasted_iota(jnp.int32, (row_count, row_count), 0)
    cols_iota = lax.broadcasted_iota(jnp.int32, (row_count, row_count), 1)
    same_seg = (rows_iota >= cols_iota) & (counts[:, None] == counts[None, :])
    log_gap = cumulative.T[:, :, None] - cumulative.T[:, None, :]
    fading = jnp.where(same_seg[None], jnp.exp(jnp.minimum(log_gap, 0.0)), 0.0)
    mixing = jnp.repeat(scores, per_group, axis=0) * fading * dt_rows.T[:, None, :]
    within = jnp.einsum('hts,shp->thp', mixing, x_conv.reshape(row_count, head_count, -1), precision=highest)
    c_heads = jnp.repeat(c_groups, per_group, axis=1)
    carried = jnp.einsum('thn,hpn->thp', c_heads, start_state, precision=highest)
    reach_decay = jnp.exp(cumulative) * jnp.where(counts == 0.0, 1.0, 0.0)[:, None]
    return (within + carried * reach_decay[:, :, None]).reshape(row_count, -1)

def reference(x_in, b_in, c_in, z_in, dt_raw, conv_x, conv_b, conv_c, decay_rate, dt_bias, skip_scale, norm_gain, w_value, resets, bucket, return_table):
    per_group = HEADS // GROUPS
    reset_real = resets.astype(jnp.float32)
    seen_flags = seen_resets(reset_real)
    block_total = SEQ // BLOCK
    emit = jax.checkpoint(partial(block_output, per_group=per_group))

    def split_blocks(array):
        return array.reshape((block_total, BLOCK) + array.shape[1:])

    def padded(array):
        return jnp.concatenate([jnp.zeros((3, array.shape[1]), jnp.float32), array], axis=0)

    def forward(x_real, b_real, c_real, z_real, dt_real):
        x_conv = conv_silu(padded(x_real), conv_x, seen_flags)
        b_conv = conv_silu(padded(b_real), conv_b, seen_flags)
        c_conv = conv_silu(padded(c_real), conv_c, seen_flags)
        dt_rows = jax.nn.softplus(dt_real + dt_bias[None, :])

        def advance(state_now, pieces):
            x_piece, b_piece, c_piece, dt_piece, reset_piece = pieces
            cumulative, counts = block_decays(dt_piece, decay_rate, reset_piece)
            output = emit(x_piece, b_piece, c_piece, dt_piece, cumulative, counts, state_now)
            state_add, block_decay = block_state(x_piece, b_piece, dt_piece, cumulative, counts, per_group)
            return (block_decay[:, None, None] * state_now + state_add, output)
        initial = jnp.zeros((HEADS, HEAD_DIM, STATE), jnp.float32)
        pieces = (split_blocks(x_conv), split_blocks(b_conv), split_blocks(c_conv), split_blocks(dt_rows), split_blocks(reset_real))
        _, outputs = lax.scan(advance, initial, pieces)
        mixed = outputs.reshape(SEQ, HEADS, HEAD_DIM) + skip_scale[None, :, None] * x_conv.reshape(SEQ, HEADS, HEAD_DIM)
        gated = mixed.reshape(SEQ, -1) * jax.nn.silu(z_real)
        norm_rms = jnp.sqrt(lax.optimization_barrier(jnp.sum(gated * gated, axis=1)) / (HEADS * HEAD_DIM) + epsilon)
        return lax.optimization_barrier(jnp.sum(gated * (norm_gain * w_value)[None, :], axis=1)) / norm_rms
    values, pull_back = jax.vjp(forward, x_in.astype(jnp.float32), b_in.astype(jnp.float32), c_in.astype(jnp.float32), z_in.astype(jnp.float32), dt_raw.astype(jnp.float32))
    value_grad = values - return_table[bucket]
    grad_x, grad_b, grad_c, grad_z, grad_dt = pull_back(value_grad)
    return (values, grad_x.astype(jnp.bfloat16), grad_b.astype(jnp.bfloat16), grad_c.astype(jnp.bfloat16), grad_z.astype(jnp.bfloat16), grad_dt.astype(jnp.bfloat16))
```

```python
import jax
import jax.numpy as jnp
from jax import lax
from jax.experimental import pallas as pl
from jax.experimental.pallas import tpu as pltpu
from jax.sharding import PartitionSpec as P

HEADS = 64
HEAD_DIM = 64
GROUPS = 4
STATE = 128
PAIR = 2 * HEAD_DIM
PAIRS_PER_GROUP = HEADS // GROUPS // 2

epsilon = 1e-05
highest = lax.Precision.HIGHEST
f32 = jnp.float32
bf16 = jnp.bfloat16


def dot(a, b, ca, cb):
    return lax.dot_general(a, b, (((ca,), (cb,)), ((), ())), preferred_element_type=f32)


def sigmoid(u):
    return 1.0 / (1.0 + jnp.exp(-u))


def conv_pre(ext, x_ref, tail_ref, w_ref, valid):
    rows = x_ref.shape[0]
    ext[0:8, :] = tail_ref[...]
    ext[8 : 8 + rows, :] = x_ref[...].astype(f32)
    total = w_ref[0:1, :] * ext[8 : 8 + rows, :]
    for k in range(1, 4):
        total = total + w_ref[k : k + 1, :] * ext[8 - k : 8 - k + rows, :] * valid[:, k - 1 : k]
    return total


def conv_back(ext, du, w_ref, valid):
    rows = du.shape[0]
    ext[...] = jnp.zeros(ext.shape, f32)
    grad = w_ref[0:1, :] * du
    head = jnp.zeros((8, du.shape[1]), f32)
    for k in range(1, 4):
        ext[8 : 8 + rows, :] = w_ref[k : k + 1, :] * du * valid[:, k - 1 : k]
        grad = grad + ext[8 + k : 8 + k + rows, :]
        head = head + ext[k : k + 8, :]
    return grad, head


def silu_back(grad, u):
    s = sigmoid(u)
    return grad * (s * (1.0 + u * (1.0 - s)))


def spread(cols, i):
    rows = cols.shape[0]
    lane = lax.broadcasted_iota(jnp.int32, (rows, PAIR), 1)
    return jnp.where(lane < HEAD_DIM, cols[:, i : i + 1], cols[:, i + 1 : i + 2])


def pair_put(*cols):
    rows = cols[0].shape[0]
    lane = lax.broadcasted_iota(jnp.int32, (rows, 8), 1)
    out = jnp.zeros((rows, 8), f32)
    for i, c in enumerate(cols):
        out = jnp.where(lane == i, c, out)
    return out


def conv_kernel(
    x, b, c, tx, tb, tc, wx, wb, wc, valid_ref, cols_ref,
    xc, bc, cc, ux, ub, uc, add, ext,
):
    k = pl.program_id(0)
    valid = valid_ref[...]

    @pl.when(lax.rem(k, PAIRS_PER_GROUP) == 0)
    def _():
        u = conv_pre(ext, b, tb, wb, valid)
        ub[...] = u
        bc[...] = (u * sigmoid(u)).astype(bf16)
        u = conv_pre(ext, c, tc, wc, valid)
        uc[...] = u
        cc[...] = (u * sigmoid(u)).astype(bf16)

    u = conv_pre(ext, x, tx, wx, valid)
    ux[...] = u
    narrow = (u * sigmoid(u)).astype(bf16)
    xc[...] = narrow
    cols = cols_ref[0]
    weighted = (narrow.astype(f32) * spread(cols, 4)).astype(bf16)
    add[...] = dot(weighted, bc[...], 0, 0).astype(bf16)


def fade(cols, rowvals, seg, j):
    gap = cols[:, j : j + 1] - rowvals[j : j + 1, :]
    return jnp.exp(jnp.minimum(gap, 0.0) + seg)


def mix_kernel(
    xc, bc, cc, z, state, cols_ref, rows_ref, seg_ref, gw, skip,
    mixed, squares, numer, scores,
):
    k = pl.program_id(0)

    @pl.when(lax.rem(k, PAIRS_PER_GROUP) == 0)
    def _():
        scores[...] = dot(cc[...], bc[...], 1, 1)

    @pl.when(k == 0)
    def _():
        squares[...] = jnp.zeros(squares.shape, f32)
        numer[...] = jnp.zeros(numer.shape, f32)

    cols = cols_ref[0]
    rowvals = rows_ref[0]
    x = xc[...]
    parts = []
    for j in range(2):
        m = scores[...] * fade(cols, rowvals, seg_ref[...], j) * rowvals[2 + j : 3 + j, :]
        parts.append(dot(m.astype(bf16), x[:, j * HEAD_DIM : (j + 1) * HEAD_DIM], 1, 0))
    within = jnp.concatenate(parts, axis=1)
    carried = dot(cc[...], state[...], 1, 1) * spread(cols, 2)
    m = within + carried + skip[...] * x.astype(f32)
    mixed[...] = m
    zz = z[...].astype(f32)
    gated = m * (zz * sigmoid(zz))
    squares[...] += gated * gated
    numer[...] += gated * gw[...]


def back_kernel(
    xc, bc, cc, z, state, cols_ref, rows_ref, seg_ref, gw, skip, mixed, vcols,
    dz, dx, dcg, dbg, ds, colout, rowout, scores, dscores, dcacc,
):
    k = pl.program_id(0)
    place = lax.rem(k, PAIRS_PER_GROUP)

    @pl.when(place == 0)
    def _():
        scores[...] = dot(cc[...], bc[...], 1, 1)
        dscores[...] = jnp.zeros(dscores.shape, f32)
        dcacc[...] = jnp.zeros(dcacc.shape, f32)

    cols = cols_ref[0]
    rowvals = rows_ref[0]
    x = xc[...]
    zz = z[...].astype(f32)
    m = mixed[...]
    s = sigmoid(zz)
    gate = zz * s
    gated = m * gate
    dgated = vcols[:, 0:1] * (gw[...] - vcols[:, 1:2] * gated)
    dz[...] = (dgated * m * (s * (1.0 + zz * (1.0 - s)))).astype(bf16)
    dy = dgated * gate
    dyb = dy.astype(bf16)
    outs = []
    rowsums = []
    colsums = []
    for j in range(2):
        sl = slice(j * HEAD_DIM, (j + 1) * HEAD_DIM)
        dt_row = rowvals[2 + j : 3 + j, :]
        f = fade(cols, rowvals, seg_ref[...], j)
        fd = f * dt_row
        sc = scores[...]
        dm = dot(dyb[:, sl], x[:, sl], 1, 1)
        outs.append(dot((sc * fd).astype(bf16), dyb[:, sl], 0, 0))
        dscores[...] += fd * dm
        q = sc * f * dm
        rowsums.append(jnp.sum(q * dt_row, axis=1, keepdims=True))
        colsums.append(jnp.sum(q, axis=0, keepdims=True))
    dx[...] = jnp.concatenate(outs, axis=1) + skip[...] * dy
    reach = dy * spread(cols, 2)
    reachb = reach.astype(bf16)
    carried = dot(cc[...], state[...], 1, 1)
    both = reach * carried
    for j in range(2):
        sl = slice(j * HEAD_DIM, (j + 1) * HEAD_DIM)
        rowsums[j] = rowsums[j] + jnp.sum(both[:, sl], axis=1, keepdims=True)
    dcacc[...] += dot(reachb, state[...], 1, 0)
    ds[...] = dot(reachb, cc[...], 0, 0).astype(bf16)
    colout[0] = pair_put(*rowsums)
    sub = lax.broadcasted_iota(jnp.int32, (8, colsums[0].shape[1]), 0)
    rowout[0] = jnp.where(sub == 0, colsums[0], jnp.where(sub == 1, colsums[1], 0.0))

    @pl.when(place == PAIRS_PER_GROUP - 1)
    def _():
        d = dscores[...].astype(bf16)
        dcg[...] = dcacc[...] + dot(d, bc[...], 1, 0)
        dbg[...] = dot(d, cc[...], 0, 0)


def last_kernel(
    xc, bc, gstate, state, cols_ref, dx, dcg, dbg, ux, ub, uc, wx, wb, wc, valid_ref,
    gx, gb, gc, hx, hb, hc, lx, lb, lc, stats, inner, dbacc, ext,
):
    k = pl.program_id(0)
    place = lax.rem(k, PAIRS_PER_GROUP)
    valid = valid_ref[...]
    rows = xc.shape[0]

    def finish(grad, u, w, out, head, last):
        g, h = conv_back(ext, silu_back(grad, u[...]), w, valid)
        out[...] = g.astype(bf16)
        head[...] = h
        last[...] = g[rows - 8 :, :]

    @pl.when(place == 0)
    def _():
        dbacc[...] = dbg[...]
        finish(dcg[...], uc, wc, gc, hc, lc)

    cols = cols_ref[0]
    x = xc[...].astype(f32)
    we = spread(cols, 4)
    g = gstate[...]
    gbx = dot(bc[...], g, 1, 1)
    xg = x * gbx
    stats[0] = pair_put(
        jnp.sum(xg[:, :HEAD_DIM], axis=1, keepdims=True),
        jnp.sum(xg[:, HEAD_DIM:], axis=1, keepdims=True),
    )
    gs = g.astype(f32) * state[...].astype(f32)
    sub = lax.broadcasted_iota(jnp.int32, (8, STATE), 0)
    inner[...] = jnp.where(
        sub == 0,
        jnp.sum(gs[:HEAD_DIM], axis=0, keepdims=True),
        jnp.where(sub == 1, jnp.sum(gs[HEAD_DIM:], axis=0, keepdims=True), 0.0),
    )[None]
    dbacc[...] += dot((x * we).astype(bf16), g, 1, 0)
    finish(dx[...] + we * gbx, ux, wx, gx, hx, lx)

    @pl.when(place == PAIRS_PER_GROUP - 1)
    def _():
        finish(dbacc[...], ub, wb, gb, hb, lb)


def shift_rows(values, amount):
    filler = jnp.zeros((amount,) + values.shape[1:], values.dtype)
    return jnp.concatenate([filler, values[: values.shape[0] - amount]], axis=0)


def hop(value, steps):
    count = lax.axis_size("ctx")
    initial, last = max(0, -steps), min(count, count - steps)
    return lax.ppermute(value, "ctx", [(i, i + steps) for i in range(initial, last)])


def carry(states, decays, sign):
    count = lax.axis_size("ctx")
    me = lax.axis_index("ctx")
    heads = decays.shape[1]
    shape3 = (heads, HEAD_DIM, STATE)
    held = hop(states, sign)
    span = 1
    while span < count - 1:
        prod = jnp.ones((heads,), f32)
        for i in range(1, span + 1):
            prod = prod * lax.dynamic_index_in_dim(
                decays, jnp.clip(me - sign * i, 0, count - 1), 0, False
            )
        got = hop(held, sign * span)
        total = prod[:, None, None] * got.astype(f32).reshape(shape3) + held.astype(f32).reshape(
            shape3
        )
        held = total.reshape(states.shape).astype(bf16)
        span *= 2
    return held


def shards(
    x_in, b_in, c_in, z_in, dt_raw, conv_x, conv_b, conv_c, decay_rate, dt_bias, skip_scale,
    norm_gain, w_value, resets, bucket, return_table,
):
    tok = x_in.shape[0]
    tp = lax.axis_index("tp")
    tpn = lax.axis_size("tp")

    def fwd(a):
        return lax.all_to_all(a, "tp", split_axis=1, concat_axis=0, tiled=True)

    def rev(a):
        return lax.all_to_all(a, "tp", split_axis=0, concat_axis=1, tiled=True)

    dt_in = fwd(dt_raw).astype(f32)
    x, b, c, z = fwd(x_in), fwd(b_in), fwd(c_in), fwd(z_in)
    T = x.shape[0]
    W, N, H = x.shape[1], b.shape[1], dt_in.shape[1]
    pairs = H // 2

    def mine(a, width):
        return lax.dynamic_slice_in_dim(a, tp * width, width, a.ndim - 1)

    wx, wb, wc = mine(conv_x, W), mine(conv_b, N), mine(conv_c, N)
    rate, bias, skip = mine(decay_rate, H), mine(dt_bias, H), mine(skip_scale, H)
    gw = mine(norm_gain * w_value, W)[None, :]
    skip_row = jnp.repeat(skip, HEAD_DIM)[None, :]

    real = resets.astype(f32)
    keep = jnp.stack([1.0 - jnp.maximum(real[-2], real[-1]), 1.0 - real[-1], jnp.ones((), f32)])
    second = jnp.maximum(real, shift_rows(real, 1))
    third = jnp.maximum(second, shift_rows(real, 2))
    valid = 1.0 - jnp.stack([real, second, third] + [real] * 5, axis=1)

    outgoing = jnp.concatenate([x[-3:], b[-3:], c[-3:]], axis=1) * keep.astype(bf16)[:, None]
    incoming = jnp.pad(hop(outgoing, 1).astype(f32), ((5, 0), (0, 0)))
    tx, tb, tc = incoming[:, :W], incoming[:, W : W + N], incoming[:, W + N :]

    dt_pre = dt_in + bias[None, :]
    dt = jax.nn.softplus(dt_pre)
    r_i = lax.broadcasted_iota(jnp.int32, (T, T), 0)
    c_i = lax.broadcasted_iota(jnp.int32, (T, T), 1)
    lower = jnp.where(r_i >= c_i, 1.0, 0.0)
    sums = jnp.dot(
        lower, jnp.concatenate([-dt * rate[None, :], real[:, None]], axis=1), precision=highest
    )
    cum, counts = sums[:, :H], jnp.round(sums[:, H])
    seg = jnp.where((r_i >= c_i) & (counts[:, None] == counts[None, :]), 0.0, -1e30)
    reach = jnp.exp(cum) * jnp.where(counts == 0.0, 1.0, 0.0)[:, None]
    tail_decay = jnp.exp(cum[-1][None, :] - cum) * jnp.where(counts == counts[-1], 1.0, 0.0)[:, None]
    we = tail_decay * dt
    decay = reach[-1]
    decays = lax.all_gather(decay, "ctx")

    def to_pairs(a):
        return a.reshape(T, pairs, 2).transpose(1, 0, 2)

    cols = jnp.concatenate([to_pairs(cum), to_pairs(reach), to_pairs(we), to_pairs(tail_decay)], 2)
    rowvals = jnp.concatenate(
        [cum.T.reshape(pairs, 2, T), dt.T.reshape(pairs, 2, T), jnp.zeros((pairs, 4, T), f32)], 1
    )

    def sds(shape, dtype=f32):
        return jax.ShapeDtypeStruct(shape, dtype)

    per = PAIRS_PER_GROUP
    px = pl.BlockSpec((T, PAIR), lambda k: (0, k))
    pg = pl.BlockSpec((T, STATE), lambda k: (0, k // per))
    t8x = pl.BlockSpec((8, PAIR), lambda k: (0, k))
    t8g = pl.BlockSpec((8, STATE), lambda k: (0, k // per))
    w4x = pl.BlockSpec((4, PAIR), lambda k: (0, k))
    w4g = pl.BlockSpec((4, STATE), lambda k: (0, k // per))
    r1x = pl.BlockSpec((1, PAIR), lambda k: (0, k))
    v8 = pl.BlockSpec((T, 8), lambda k: (0, 0))
    c8 = pl.BlockSpec((1, T, 8), lambda k: (k, 0, 0))
    r8 = pl.BlockSpec((1, 8, T), lambda k: (k, 0, 0))
    st = pl.BlockSpec((PAIR, STATE), lambda k: (k, 0))
    tt = pl.BlockSpec((T, T), lambda k: (0, 0))
    acc = pl.BlockSpec((T, PAIR), lambda k: (0, 0))
    params = pltpu.CompilerParams(
        dimension_semantics=("arbitrary",), vmem_limit_bytes=32 * 1024 * 1024
    )
    ext = pltpu.VMEM((T + 16, PAIR), f32)
    square = pltpu.VMEM((T, T), f32)

    xc, bc, cc, ux, ub, uc, add = pl.pallas_call(
        conv_kernel,
        grid=(pairs,),
        in_specs=[px, pg, pg, t8x, t8g, t8g, w4x, w4g, w4g, v8, c8],
        out_specs=[px, pg, pg, px, pg, pg, st],
        out_shape=[
            sds((T, W), bf16), sds((T, N), bf16), sds((T, N), bf16),
            sds((T, W)), sds((T, N)), sds((T, N)), sds((W, STATE), bf16),
        ],
        scratch_shapes=[ext],
        compiler_params=params,
    )(x, b, c, tx, tb, tc, wx, wb, wc, valid, cols)

    state = carry(add, decays, 1)

    mixed, squares, numer = pl.pallas_call(
        mix_kernel,
        grid=(pairs,),
        in_specs=[px, pg, pg, px, st, c8, r8, tt, r1x, r1x],
        out_specs=[px, acc, acc],
        out_shape=[sds((T, W)), sds((T, PAIR)), sds((T, PAIR))],
        scratch_shapes=[square],
        compiler_params=params,
    )(xc, bc, cc, z, state, cols, rowvals, seg, gw, skip_row)

    both = lax.psum(jnp.stack([jnp.sum(squares, axis=1), jnp.sum(numer, axis=1)]), "tp")
    width_all = W * tpn
    rms = jnp.sqrt(both[0] / width_all + epsilon)
    values = both[1] / rms
    table_n = return_table.shape[0]
    onehot = bucket[:, None] == lax.broadcasted_iota(jnp.int32, (1, table_n), 1)
    target = jnp.sum(jnp.where(onehot, return_table[None, :], 0.0), axis=1)
    vscale = (values - target) / rms
    vcols = jnp.stack([vscale, values / (rms * width_all)] + [vscale] * 6, axis=1)

    dz, dx, dcg, dbg, ds, colout, rowout = pl.pallas_call(
        back_kernel,
        grid=(pairs,),
        in_specs=[px, pg, pg, px, st, c8, r8, tt, r1x, r1x, px, v8],
        out_specs=[px, px, pg, pg, st, c8, r8],
        out_shape=[
            sds((T, W), bf16), sds((T, W)), sds((T, N)), sds((T, N)), sds((W, STATE), bf16),
            sds((pairs, T, 8)), sds((pairs, 8, T)),
        ],
        scratch_shapes=[square, square, pltpu.VMEM((T, STATE), f32)],
        compiler_params=params,
    )(xc, bc, cc, z, state, cols, rowvals, seg, gw, skip_row, mixed, vcols)

    grad_z = rev(dz)
    gstate = carry(ds, decays, -1)

    gx, gb, gc, hx, hb, hc, lx, lb, lc, stats, inner = pl.pallas_call(
        last_kernel,
        grid=(pairs,),
        in_specs=[px, pg, st, st, c8, px, pg, pg, px, pg, pg, w4x, w4g, w4g, v8],
        out_specs=[px, pg, pg, t8x, t8g, t8g, t8x, t8g, t8g, c8, r8s(STATE)],
        out_shape=[
            sds((T, W), bf16), sds((T, N), bf16), sds((T, N), bf16),
            sds((8, W)), sds((8, N)), sds((8, N)), sds((8, W)), sds((8, N)), sds((8, N)),
            sds((pairs, T, 8)), sds((pairs, 8, STATE)),
        ],
        scratch_shapes=[pltpu.VMEM((T, STATE), f32), ext],
        compiler_params=params,
    )(xc, bc, gstate, state, cols, dx, dcg, dbg, ux, ub, uc, wx, wb, wc, valid)

    def from_cols(a):
        return a[:, :, :2].transpose(1, 0, 2).reshape(T, H)

    row_part = from_cols(colout)
    col_sum = rowout[:, :2, :].reshape(H, T).T
    xg = from_cols(stats)
    ginner = jnp.sum(inner[:, :2, :], axis=2).reshape(H)
    tail_part = we * xg
    dcum = row_part - dt * col_sum - tail_part
    at_end = jnp.sum(tail_part, axis=0) + decay * ginner
    rev_sum = jnp.dot(lower.T, dcum, precision=highest) + at_end[None, :]
    ddt = col_sum + tail_decay * xg - rate[None, :] * rev_sum
    grad_dt = rev((ddt * jax.nn.sigmoid(dt_pre)).astype(bf16))

    heads3 = jnp.concatenate([hx, hb, hc], axis=1)[5:8]
    last3 = jnp.concatenate([lx, lb, lc], axis=1)[5:8]
    fixed = (last3 + hop(heads3, -1) * keep[:, None]).astype(bf16)
    gx = lax.dynamic_update_slice(gx, fixed[:, :W], (T - 3, 0))
    gb = lax.dynamic_update_slice(gb, fixed[:, W : W + N], (T - 3, 0))
    gc = lax.dynamic_update_slice(gc, fixed[:, W + N :], (T - 3, 0))
    out_values = lax.dynamic_slice_in_dim(values, tp * tok, tok, 0)
    return (out_values, rev(gx), rev(gb), rev(gc), grad_z, grad_dt)


def r8s(width):
    return pl.BlockSpec((1, 8, width), lambda k: (k, 0, 0))


def solution(mesh):
    row = P(("group", "ctx", "tp"), None)
    seq = P(("group", "ctx"))
    return jax.shard_map(
        shards,
        mesh=mesh,
        in_specs=(row,) * 5 + (P(),) * 8 + (seq, seq, P()),
        out_specs=(P(("group", "ctx", "tp")),) + (row,) * 5,
        check_vma=False,
    )
```

```python
from functools import partial

import jax
import jax.numpy as jnp
from jax import lax
from jax.experimental import pallas as pl
from jax.experimental.pallas import tpu as pltpu
from jax.sharding import PartitionSpec as P

HEADS = 64
HEAD_DIM = 64
GROUPS = 4
STATE = 128
PAIR = 2 * HEAD_DIM
PAIRS_PER_GROUP = HEADS // GROUPS // 2

epsilon = 1e-05
highest = lax.Precision.HIGHEST
f32 = jnp.float32
bf16 = jnp.bfloat16


def dot(a, b, ca, cb):
    return lax.dot_general(a, b, (((ca,), (cb,)), ((), ())), preferred_element_type=f32)


def sigmoid(u):
    return 1.0 / (1.0 + jnp.exp(-u))


def conv_pre(ext, x_ref, tail_ref, w_ref, valid):
    rows = x_ref.shape[0]
    ext[0:8, :] = tail_ref[...]
    ext[8 : 8 + rows, :] = x_ref[...].astype(f32)
    total = w_ref[0:1, :] * ext[8 : 8 + rows, :]
    for k in range(1, 4):
        total = total + w_ref[k : k + 1, :] * ext[8 - k : 8 - k + rows, :] * valid[:, k - 1 : k]
    return total


def conv_back(ext, du, w_ref, valid):
    rows = du.shape[0]
    ext[...] = jnp.zeros(ext.shape, f32)
    grad = w_ref[0:1, :] * du
    head = jnp.zeros((8, du.shape[1]), f32)
    for k in range(1, 4):
        ext[8 : 8 + rows, :] = w_ref[k : k + 1, :] * du * valid[:, k - 1 : k]
        grad = grad + ext[8 + k : 8 + k + rows, :]
        head = head + ext[k : k + 8, :]
    return grad, head


def silu_back(grad, u):
    s = sigmoid(u)
    return grad * (s * (1.0 + u * (1.0 - s)))


def spread(cols, i):
    rows = cols.shape[0]
    lane = lax.broadcasted_iota(jnp.int32, (rows, PAIR), 1)
    return jnp.where(lane < HEAD_DIM, cols[:, i : i + 1], cols[:, i + 1 : i + 2])


def pair_put(*cols):
    rows = cols[0].shape[0]
    lane = lax.broadcasted_iota(jnp.int32, (rows, 8), 1)
    out = jnp.zeros((rows, 8), f32)
    for i, c in enumerate(cols):
        out = jnp.where(lane == i, c, out)
    return out


def conv_kernel(
    x, b, c, tx, tb, tc, wx, wb, wc, valid_ref, cols_ref,
    xc, bc, cc, ux, ub, uc, add, ext,
):
    k = pl.program_id(0)
    valid = valid_ref[...]

    @pl.when(lax.rem(k, PAIRS_PER_GROUP) == 0)
    def _():
        u = conv_pre(ext, b, tb, wb, valid)
        ub[...] = u
        bc[...] = (u * sigmoid(u)).astype(bf16)
        u = conv_pre(ext, c, tc, wc, valid)
        uc[...] = u
        cc[...] = (u * sigmoid(u)).astype(bf16)

    u = conv_pre(ext, x, tx, wx, valid)
    ux[...] = u
    narrow = (u * sigmoid(u)).astype(bf16)
    xc[...] = narrow
    cols = cols_ref[0]
    weighted = (narrow.astype(f32) * spread(cols, 4)).astype(bf16)
    add[...] = dot(weighted, bc[...], 0, 0).astype(bf16)


def fade(cols, rowvals, seg, j):
    gap = cols[:, j : j + 1] - rowvals[j : j + 1, :]
    return jnp.exp(jnp.minimum(gap, 0.0) + seg)


def mix_kernel(
    xc, bc, cc, z, state, cols_ref, rows_ref, seg_ref, gw, skip,
    mixed, squares, numer, scores,
):
    k = pl.program_id(0)

    @pl.when(lax.rem(k, PAIRS_PER_GROUP) == 0)
    def _():
        scores[...] = dot(cc[...], bc[...], 1, 1)

    @pl.when(k == 0)
    def _():
        squares[...] = jnp.zeros(squares.shape, f32)
        numer[...] = jnp.zeros(numer.shape, f32)

    cols = cols_ref[0]
    rowvals = rows_ref[0]
    x = xc[...]
    parts = []
    for j in range(2):
        m = scores[...] * fade(cols, rowvals, seg_ref[...], j) * rowvals[2 + j : 3 + j, :]
        parts.append(dot(m.astype(bf16), x[:, j * HEAD_DIM : (j + 1) * HEAD_DIM], 1, 0))
    within = jnp.concatenate(parts, axis=1)
    carried = dot(cc[...], state[...], 1, 1) * spread(cols, 2)
    m = within + carried + skip[...] * x.astype(f32)
    mixed[...] = m
    zz = z[...].astype(f32)
    gated = m * (zz * sigmoid(zz))
    squares[...] += gated * gated
    numer[...] += gated * gw[...]


def back_kernel(
    xc, bc, cc, z, state, cols_ref, rows_ref, seg_ref, gw, skip, mixed, vcols,
    dz, dx, dcg, dbg, ds, colout, rowout, scores, dscores, dcacc,
):
    k = pl.program_id(0)
    place = lax.rem(k, PAIRS_PER_GROUP)

    @pl.when(place == 0)
    def _():
        scores[...] = dot(cc[...], bc[...], 1, 1)
        dscores[...] = jnp.zeros(dscores.shape, f32)
        dcacc[...] = jnp.zeros(dcacc.shape, f32)

    cols = cols_ref[0]
    rowvals = rows_ref[0]
    x = xc[...]
    zz = z[...].astype(f32)
    m = mixed[...]
    s = sigmoid(zz)
    gate = zz * s
    gated = m * gate
    dgated = vcols[:, 0:1] * (gw[...] - vcols[:, 1:2] * gated)
    dz[...] = (dgated * m * (s * (1.0 + zz * (1.0 - s)))).astype(bf16)
    dy = dgated * gate
    dyb = dy.astype(bf16)
    outs = []
    rowsums = []
    colsums = []
    for j in range(2):
        sl = slice(j * HEAD_DIM, (j + 1) * HEAD_DIM)
        dt_row = rowvals[2 + j : 3 + j, :]
        f = fade(cols, rowvals, seg_ref[...], j)
        fd = f * dt_row
        sc = scores[...]
        dm = dot(dyb[:, sl], x[:, sl], 1, 1)
        outs.append(dot((sc * fd).astype(bf16), dyb[:, sl], 0, 0))
        dscores[...] += fd * dm
        q = sc * f * dm
        rowsums.append(jnp.sum(q * dt_row, axis=1, keepdims=True))
        colsums.append(jnp.sum(q, axis=0, keepdims=True))
    dx[...] = jnp.concatenate(outs, axis=1) + skip[...] * dy
    reach = dy * spread(cols, 2)
    reachb = reach.astype(bf16)
    carried = dot(cc[...], state[...], 1, 1)
    both = reach * carried
    for j in range(2):
        sl = slice(j * HEAD_DIM, (j + 1) * HEAD_DIM)
        rowsums[j] = rowsums[j] + jnp.sum(both[:, sl], axis=1, keepdims=True)
    dcacc[...] += dot(reachb, state[...], 1, 0)
    ds[...] = dot(reachb, cc[...], 0, 0).astype(bf16)
    colout[0] = pair_put(*rowsums)
    sub = lax.broadcasted_iota(jnp.int32, (8, colsums[0].shape[1]), 0)
    rowout[0] = jnp.where(sub == 0, colsums[0], jnp.where(sub == 1, colsums[1], 0.0))

    @pl.when(place == PAIRS_PER_GROUP - 1)
    def _():
        d = dscores[...].astype(bf16)
        dcg[...] = dcacc[...] + dot(d, bc[...], 1, 0)
        dbg[...] = dot(d, cc[...], 0, 0)


def last_kernel(
    xc, bc, gstate, state, cols_ref, dx, dcg, dbg, ux, ub, uc, wx, wb, wc, valid_ref,
    gx, gb, gc, hx, hb, hc, lx, lb, lc, stats, inner, dbacc, ext,
):
    k = pl.program_id(0)
    place = lax.rem(k, PAIRS_PER_GROUP)
    valid = valid_ref[...]
    rows = xc.shape[0]

    def finish(grad, u, w, out, head, last):
        g, h = conv_back(ext, silu_back(grad, u[...]), w, valid)
        out[...] = g.astype(bf16)
        head[...] = h
        last[...] = g[rows - 8 :, :]

    @pl.when(place == 0)
    def _():
        dbacc[...] = dbg[...]
        finish(dcg[...], uc, wc, gc, hc, lc)

    cols = cols_ref[0]
    x = xc[...].astype(f32)
    we = spread(cols, 4)
    g = gstate[...]
    gbx = dot(bc[...], g, 1, 1)
    xg = x * gbx
    stats[0] = pair_put(
        jnp.sum(xg[:, :HEAD_DIM], axis=1, keepdims=True),
        jnp.sum(xg[:, HEAD_DIM:], axis=1, keepdims=True),
    )
    gs = g.astype(f32) * state[...].astype(f32)
    sub = lax.broadcasted_iota(jnp.int32, (8, STATE), 0)
    inner[...] = jnp.where(
        sub == 0,
        jnp.sum(gs[:HEAD_DIM], axis=0, keepdims=True),
        jnp.where(sub == 1, jnp.sum(gs[HEAD_DIM:], axis=0, keepdims=True), 0.0),
    )[None]
    dbacc[...] += dot((x * we).astype(bf16), g, 1, 0)
    finish(dx[...] + we * gbx, ux, wx, gx, hx, lx)

    @pl.when(place == PAIRS_PER_GROUP - 1)
    def _():
        finish(dbacc[...], ub, wb, gb, hb, lb)


def shift_rows(values, amount):
    filler = jnp.zeros((amount,) + values.shape[1:], values.dtype)
    return jnp.concatenate([filler, values[: values.shape[0] - amount]], axis=0)


def hop(value, steps):
    count = lax.axis_size("ctx")
    initial, last = max(0, -steps), min(count, count - steps)
    return lax.ppermute(value, "ctx", [(i, i + steps) for i in range(initial, last)])


MESH = pl.DeviceIdType.MESH
CHUNKS = 4


def carry_kernel(sign, count, s_ref, mine_ref, peer_ref, out, other, came, going, sems):
    me = lax.axis_index("ctx")
    half = lax.rem(me, 2)
    pair = lax.div(me, 2)
    pairs = count // 2
    peer = me + 1 - 2 * half
    is_first = half == (0 if sign > 0 else 1)
    has_prev = (pair > 0) if sign > 0 else (pair < pairs - 1)
    has_next = (pair < pairs - 1) if sign > 0 else (pair > 0)
    heads = s_ref.shape[0]
    step = heads // CHUNKS

    barrier = pltpu.get_barrier_semaphore()
    pl.semaphore_signal(barrier, inc=1, device_id={"ctx": peer}, device_id_type=MESH)

    @pl.when(has_prev)
    def _():
        pl.semaphore_signal(barrier, inc=1, device_id={"ctx": me - 2 * sign}, device_id_type=MESH)

    @pl.when(has_next)
    def _():
        pl.semaphore_signal(barrier, inc=1, device_id={"ctx": me + 2 * sign}, device_id_type=MESH)

    pl.semaphore_wait(barrier, 1 + jnp.where(has_prev, 1, 0) + jnp.where(has_next, 1, 0))

    def swap(i):
        part = pl.ds(i * step, step)
        return pltpu.make_async_remote_copy(
            src_ref=s_ref.at[part], dst_ref=other.at[part], send_sem=sems.at[0, i],
            recv_sem=sems.at[1, i], device_id={"ctx": peer}, device_id_type=MESH,
        )

    def chain(i):
        part = pl.ds(i * step, step)
        return pltpu.make_async_remote_copy(
            src_ref=going.at[part], dst_ref=came.at[part], send_sem=sems.at[2, i],
            recv_sem=sems.at[3, i], device_id={"ctx": me + 2 * sign}, device_id_type=MESH,
        )

    for i in range(CHUNKS):
        swap(i).start()

    @pl.when(jnp.logical_not(has_prev))
    def _():
        came[...] = jnp.zeros(came.shape, bf16)

    for i in range(CHUNKS):
        part = slice(i * step, (i + 1) * step)
        swap(i).wait_recv()

        @pl.when(has_prev)
        def _():
            chain(i).wait_recv()

        base = came[part].astype(f32)
        own, got = s_ref[part].astype(f32), other[part].astype(f32)
        d_own, d_got = mine_ref[part], peer_ref[part]

        @pl.when(is_first)
        def _():
            out[part] = came[part]
            going[part] = (d_got * (d_own * base + own) + got).astype(bf16)

        @pl.when(jnp.logical_not(is_first))
        def _():
            mid = d_got * base + got
            out[part] = mid.astype(bf16)
            going[part] = (d_own * mid + own).astype(bf16)

        @pl.when(has_next)
        def _():
            chain(i).start()

    for i in range(CHUNKS):
        swap(i).wait_send()

        @pl.when(has_next)
        def _():
            chain(i).wait_send()


def carry(states, mine_decay, peer_decay, sign):
    count = lax.axis_size("ctx")
    heads = states.shape[0] // HEAD_DIM
    shape = (heads, HEAD_DIM, STATE)
    vmem = pl.BlockSpec(memory_space=pltpu.VMEM)
    out = pl.pallas_call(
        partial(carry_kernel, sign, count),
        out_shape=jax.ShapeDtypeStruct(shape, bf16),
        in_specs=[vmem] * 3,
        out_specs=vmem,
        scratch_shapes=[
            pltpu.VMEM(shape, bf16), pltpu.VMEM(shape, bf16), pltpu.VMEM(shape, bf16),
            pltpu.SemaphoreType.DMA((4, CHUNKS)),
        ],
        compiler_params=pltpu.CompilerParams(
            collective_id=0 if sign > 0 else 1, has_side_effects=True,
            vmem_limit_bytes=32 * 1024 * 1024,
        ),
    )(states.reshape(shape), mine_decay, peer_decay)
    return out.reshape(states.shape)


def swap_barrier(peer):
    barrier = pltpu.get_barrier_semaphore()
    pl.semaphore_signal(barrier, inc=1, device_id={"tp": peer}, device_id_type=MESH)
    pl.semaphore_wait(barrier, 1)


def move_kernel(to_heads, count, *refs):
    ins, outs, sems = refs[:count], refs[count : 2 * count], refs[2 * count]
    me = lax.axis_index("tp")
    peer = 1 - me
    swap_barrier(peer)
    copies = []
    for i in range(count):
        a, o = ins[i], outs[i]
        if to_heads:
            rows, width = a.shape[0], o.shape[1]
            there = pl.ds(pl.multiple_of(peer * width, 128), width)
            here = pl.ds(pl.multiple_of(me * width, 128), width)
            place = pl.ds(pl.multiple_of(me * rows, 8), rows)
            send, keep, dst = a.at[:, there], a.at[:, here], o.at[place, :]
        else:
            rows, width = o.shape[0], a.shape[1]
            there = pl.ds(pl.multiple_of(peer * rows, 8), rows)
            here = pl.ds(pl.multiple_of(me * rows, 8), rows)
            place = pl.ds(pl.multiple_of(me * width, 128), width)
            send, keep, dst = a.at[there, :], a.at[here, :], o.at[:, place]
        away = pltpu.make_async_remote_copy(
            src_ref=send, dst_ref=dst, send_sem=sems.at[0, i], recv_sem=sems.at[1, i],
            device_id={"tp": peer}, device_id_type=MESH,
        )
        away.start()
        local = pltpu.make_async_copy(keep, dst, sems.at[2, i])
        local.start()
        copies.append((away, local))
    for away, local in copies:
        away.wait()
        local.wait()


def move(arrays, to_heads, collective):
    count = len(arrays)
    anywhere = pl.BlockSpec(memory_space=pl.ANY)
    shapes = []
    for a in arrays:
        r, w = a.shape
        shapes.append(jax.ShapeDtypeStruct((2 * r, w // 2) if to_heads else (r // 2, 2 * w), a.dtype))
    return pl.pallas_call(
        partial(move_kernel, to_heads, count),
        out_shape=shapes,
        in_specs=[anywhere] * count,
        out_specs=[anywhere] * count,
        scratch_shapes=[pltpu.SemaphoreType.DMA((3, count))],
        compiler_params=pltpu.CompilerParams(collective_id=collective, has_side_effects=True),
    )(*arrays)


def shards(
    x_in, b_in, c_in, z_in, dt_raw, conv_x, conv_b, conv_c, decay_rate, dt_bias, skip_scale,
    norm_gain, w_value, resets, bucket, return_table,
):
    tok = x_in.shape[0]
    tp = lax.axis_index("tp")
    tpn = lax.axis_size("tp")

    part_heads = dt_raw.shape[1] // tpn
    lanes = ((0, 0), (0, 128 - part_heads))
    dt_wide = jnp.concatenate(
        [jnp.pad(dt_raw[:, :part_heads], lanes), jnp.pad(dt_raw[:, part_heads:], lanes)], axis=1
    )
    x, b, c, z, dt_got = move([x_in, b_in, c_in, z_in, dt_wide], True, 2)
    dt_in = dt_got[:, :part_heads].astype(f32)
    T = x.shape[0]
    W, N, H = x.shape[1], b.shape[1], dt_in.shape[1]
    pairs = H // 2

    def mine(a, width):
        return lax.dynamic_slice_in_dim(a, tp * width, width, a.ndim - 1)

    wx, wb, wc = mine(conv_x, W), mine(conv_b, N), mine(conv_c, N)
    rate, bias, skip = mine(decay_rate, H), mine(dt_bias, H), mine(skip_scale, H)
    gw = mine(norm_gain * w_value, W)[None, :]
    skip_row = jnp.repeat(skip, HEAD_DIM)[None, :]

    real = resets.astype(f32)
    keep = jnp.stack([1.0 - jnp.maximum(real[-2], real[-1]), 1.0 - real[-1], jnp.ones((), f32)])
    second = jnp.maximum(real, shift_rows(real, 1))
    third = jnp.maximum(second, shift_rows(real, 2))
    valid = 1.0 - jnp.stack([real, second, third] + [real] * 5, axis=1)

    outgoing = jnp.concatenate([x[-3:], b[-3:], c[-3:]], axis=1) * keep.astype(bf16)[:, None]
    incoming = jnp.pad(hop(outgoing, 1).astype(f32), ((5, 0), (0, 0)))
    tx, tb, tc = incoming[:, :W], incoming[:, W : W + N], incoming[:, W + N :]

    dt_pre = dt_in + bias[None, :]
    dt = jax.nn.softplus(dt_pre)
    r_i = lax.broadcasted_iota(jnp.int32, (T, T), 0)
    c_i = lax.broadcasted_iota(jnp.int32, (T, T), 1)
    lower = jnp.where(r_i >= c_i, 1.0, 0.0)
    sums = jnp.dot(
        lower, jnp.concatenate([-dt * rate[None, :], real[:, None]], axis=1), precision=highest
    )
    cum, counts = sums[:, :H], jnp.round(sums[:, H])
    seg = jnp.where((r_i >= c_i) & (counts[:, None] == counts[None, :]), 0.0, -1e30)
    reach = jnp.exp(cum) * jnp.where(counts == 0.0, 1.0, 0.0)[:, None]
    tail_decay = jnp.exp(cum[-1][None, :] - cum) * jnp.where(counts == counts[-1], 1.0, 0.0)[:, None]
    we = tail_decay * dt
    decay = reach[-1]
    count = lax.axis_size("ctx")
    peer = lax.ppermute(decay, "ctx", [(i, i ^ 1) for i in range(count)])
    mine_decay = jnp.broadcast_to(decay[:, None, None], (H, 1, STATE))
    peer_decay = jnp.broadcast_to(peer[:, None, None], (H, 1, STATE))

    def to_pairs(a):
        return a.reshape(T, pairs, 2).transpose(1, 0, 2)

    cols = jnp.concatenate([to_pairs(cum), to_pairs(reach), to_pairs(we), to_pairs(tail_decay)], 2)
    rowvals = jnp.concatenate(
        [cum.T.reshape(pairs, 2, T), dt.T.reshape(pairs, 2, T), jnp.zeros((pairs, 4, T), f32)], 1
    )

    def sds(shape, dtype=f32):
        return jax.ShapeDtypeStruct(shape, dtype)

    per = PAIRS_PER_GROUP
    px = pl.BlockSpec((T, PAIR), lambda k: (0, k))
    pg = pl.BlockSpec((T, STATE), lambda k: (0, k // per))
    t8x = pl.BlockSpec((8, PAIR), lambda k: (0, k))
    t8g = pl.BlockSpec((8, STATE), lambda k: (0, k // per))
    w4x = pl.BlockSpec((4, PAIR), lambda k: (0, k))
    w4g = pl.BlockSpec((4, STATE), lambda k: (0, k // per))
    r1x = pl.BlockSpec((1, PAIR), lambda k: (0, k))
    v8 = pl.BlockSpec((T, 8), lambda k: (0, 0))
    c8 = pl.BlockSpec((1, T, 8), lambda k: (k, 0, 0))
    r8 = pl.BlockSpec((1, 8, T), lambda k: (k, 0, 0))
    st = pl.BlockSpec((PAIR, STATE), lambda k: (k, 0))
    tt = pl.BlockSpec((T, T), lambda k: (0, 0))
    acc = pl.BlockSpec((T, PAIR), lambda k: (0, 0))
    params = pltpu.CompilerParams(
        dimension_semantics=("arbitrary",), vmem_limit_bytes=32 * 1024 * 1024
    )
    ext = pltpu.VMEM((T + 16, PAIR), f32)
    square = pltpu.VMEM((T, T), f32)

    xc, bc, cc, ux, ub, uc, add = pl.pallas_call(
        conv_kernel,
        grid=(pairs,),
        in_specs=[px, pg, pg, t8x, t8g, t8g, w4x, w4g, w4g, v8, c8],
        out_specs=[px, pg, pg, px, pg, pg, st],
        out_shape=[
            sds((T, W), bf16), sds((T, N), bf16), sds((T, N), bf16),
            sds((T, W)), sds((T, N)), sds((T, N)), sds((W, STATE), bf16),
        ],
        scratch_shapes=[ext],
        compiler_params=params,
    )(x, b, c, tx, tb, tc, wx, wb, wc, valid, cols)

    state = carry(add, mine_decay, peer_decay, 1)

    mixed, squares, numer = pl.pallas_call(
        mix_kernel,
        grid=(pairs,),
        in_specs=[px, pg, pg, px, st, c8, r8, tt, r1x, r1x],
        out_specs=[px, acc, acc],
        out_shape=[sds((T, W)), sds((T, PAIR)), sds((T, PAIR))],
        scratch_shapes=[square],
        compiler_params=params,
    )(xc, bc, cc, z, state, cols, rowvals, seg, gw, skip_row)

    both = lax.psum(jnp.stack([jnp.sum(squares, axis=1), jnp.sum(numer, axis=1)]), "tp")
    width_all = W * tpn
    rms = jnp.sqrt(both[0] / width_all + epsilon)
    values = both[1] / rms
    table_n = return_table.shape[0]
    onehot = bucket[:, None] == lax.broadcasted_iota(jnp.int32, (1, table_n), 1)
    target = jnp.sum(jnp.where(onehot, return_table[None, :], 0.0), axis=1)
    vscale = (values - target) / rms
    vcols = jnp.stack([vscale, values / (rms * width_all)] + [vscale] * 6, axis=1)

    dz, dx, dcg, dbg, ds, colout, rowout = pl.pallas_call(
        back_kernel,
        grid=(pairs,),
        in_specs=[px, pg, pg, px, st, c8, r8, tt, r1x, r1x, px, v8],
        out_specs=[px, px, pg, pg, st, c8, r8],
        out_shape=[
            sds((T, W), bf16), sds((T, W)), sds((T, N)), sds((T, N)), sds((W, STATE), bf16),
            sds((pairs, T, 8)), sds((pairs, 8, T)),
        ],
        scratch_shapes=[square, square, pltpu.VMEM((T, STATE), f32)],
        compiler_params=params,
    )(xc, bc, cc, z, state, cols, rowvals, seg, gw, skip_row, mixed, vcols)

    gstate = carry(ds, mine_decay, peer_decay, -1)

    gx, gb, gc, hx, hb, hc, lx, lb, lc, stats, inner = pl.pallas_call(
        last_kernel,
        grid=(pairs,),
        in_specs=[px, pg, st, st, c8, px, pg, pg, px, pg, pg, w4x, w4g, w4g, v8],
        out_specs=[px, pg, pg, t8x, t8g, t8g, t8x, t8g, t8g, c8, r8s(STATE)],
        out_shape=[
            sds((T, W), bf16), sds((T, N), bf16), sds((T, N), bf16),
            sds((8, W)), sds((8, N)), sds((8, N)), sds((8, W)), sds((8, N)), sds((8, N)),
            sds((pairs, T, 8)), sds((pairs, 8, STATE)),
        ],
        scratch_shapes=[pltpu.VMEM((T, STATE), f32), ext],
        compiler_params=params,
    )(xc, bc, gstate, state, cols, dx, dcg, dbg, ux, ub, uc, wx, wb, wc, valid)

    def from_cols(a):
        return a[:, :, :2].transpose(1, 0, 2).reshape(T, H)

    row_part = from_cols(colout)
    col_sum = rowout[:, :2, :].reshape(H, T).T
    xg = from_cols(stats)
    ginner = jnp.sum(inner[:, :2, :], axis=2).reshape(H)
    tail_part = we * xg
    dcum = row_part - dt * col_sum - tail_part
    at_end = jnp.sum(tail_part, axis=0) + decay * ginner
    rev_sum = jnp.dot(lower.T, dcum, precision=highest) + at_end[None, :]
    ddt = col_sum + tail_decay * xg - rate[None, :] * rev_sum
    ddt_wide = jnp.pad((ddt * jax.nn.sigmoid(dt_pre)).astype(bf16), lanes)

    heads3 = jnp.concatenate([hx, hb, hc], axis=1)[5:8]
    last3 = jnp.concatenate([lx, lb, lc], axis=1)[5:8]
    fixed = (last3 + hop(heads3, -1) * keep[:, None]).astype(bf16)
    gx = lax.dynamic_update_slice(gx, fixed[:, :W], (T - 3, 0))
    gb = lax.dynamic_update_slice(gb, fixed[:, W : W + N], (T - 3, 0))
    gc = lax.dynamic_update_slice(gc, fixed[:, W + N :], (T - 3, 0))
    out_values = lax.dynamic_slice_in_dim(values, tp * tok, tok, 0)
    grad_x, grad_b, grad_c, grad_z, dt_out = move([gx, gb, gc, dz, ddt_wide], False, 3)
    grad_dt = jnp.concatenate([dt_out[:, :part_heads], dt_out[:, 128 : 128 + part_heads]], axis=1)
    return (out_values, grad_x, grad_b, grad_c, grad_z, grad_dt)


def r8s(width):
    return pl.BlockSpec((1, 8, width), lambda k: (k, 0, 0))


def solution(mesh):
    row = P(("group", "ctx", "tp"), None)
    seq = P(("group", "ctx"))
    return jax.shard_map(
        shards,
        mesh=mesh,
        in_specs=(row,) * 5 + (P(),) * 8 + (seq, seq, P()),
        out_specs=(P(("group", "ctx", "tp")),) + (row,) * 5,
        check_vma=False,
    )
```

```python
from functools import partial

import jax
import jax.numpy as jnp
from jax import lax
from jax.experimental import pallas as pl
from jax.experimental.pallas import tpu as pltpu
from jax.sharding import PartitionSpec as P

HEADS = 64
HEAD_DIM = 64
GROUPS = 4
STATE = 128
PAIR = 2 * HEAD_DIM
PAIRS_PER_GROUP = HEADS // GROUPS // 2

epsilon = 1e-05
highest = lax.Precision.HIGHEST
f32 = jnp.float32
bf16 = jnp.bfloat16


def dot(a, b, ca, cb):
    return lax.dot_general(a, b, (((ca,), (cb,)), ((), ())), preferred_element_type=f32)


def sigmoid(u):
    return 1.0 / (1.0 + jnp.exp(-u))


def conv_pre(ext, x_ref, tail_ref, w_ref, valid):
    rows = x_ref.shape[0]
    ext[0:8, :] = tail_ref[...]
    ext[8 : 8 + rows, :] = x_ref[...].astype(f32)
    total = w_ref[0:1, :] * ext[8 : 8 + rows, :]
    for k in range(1, 4):
        total = total + w_ref[k : k + 1, :] * ext[8 - k : 8 - k + rows, :] * valid[:, k - 1 : k]
    return total


def conv_back(ext, du, w_ref, valid):
    rows = du.shape[0]
    ext[...] = jnp.zeros(ext.shape, f32)
    grad = w_ref[0:1, :] * du
    head = jnp.zeros((8, du.shape[1]), f32)
    for k in range(1, 4):
        ext[8 : 8 + rows, :] = w_ref[k : k + 1, :] * du * valid[:, k - 1 : k]
        grad = grad + ext[8 + k : 8 + k + rows, :]
        head = head + ext[k : k + 8, :]
    return grad, head


def silu_back(grad, u):
    s = sigmoid(u)
    return grad * (s * (1.0 + u * (1.0 - s)))


def spread(cols, i):
    rows = cols.shape[0]
    lane = lax.broadcasted_iota(jnp.int32, (rows, PAIR), 1)
    return jnp.where(lane < HEAD_DIM, cols[:, i : i + 1], cols[:, i + 1 : i + 2])


def pair_put(*cols):
    rows = cols[0].shape[0]
    lane = lax.broadcasted_iota(jnp.int32, (rows, 8), 1)
    out = jnp.zeros((rows, 8), f32)
    for i, c in enumerate(cols):
        out = jnp.where(lane == i, c, out)
    return out


def conv_kernel(
    x, b, c, tx, tb, tc, wx, wb, wc, valid_ref, cols_ref,
    xc, bc, cc, ux, ub, uc, add, ext,
):
    k = pl.program_id(0)
    valid = valid_ref[...]

    @pl.when(lax.rem(k, PAIRS_PER_GROUP) == 0)
    def _():
        u = conv_pre(ext, b, tb, wb, valid)
        ub[...] = u
        bc[...] = (u * sigmoid(u)).astype(bf16)
        u = conv_pre(ext, c, tc, wc, valid)
        uc[...] = u
        cc[...] = (u * sigmoid(u)).astype(bf16)

    u = conv_pre(ext, x, tx, wx, valid)
    ux[...] = u
    narrow = (u * sigmoid(u)).astype(bf16)
    xc[...] = narrow
    cols = cols_ref[0]
    weighted = (narrow.astype(f32) * spread(cols, 4)).astype(bf16)
    add[...] = dot(weighted, bc[...], 0, 0).astype(bf16)


def fade(cols, rowvals, seg, j):
    gap = cols[:, j : j + 1] - rowvals[j : j + 1, :]
    return jnp.exp(jnp.minimum(gap, 0.0) + seg)


def mix_kernel(
    xc, bc, cc, z, state, cols_ref, rows_ref, seg_ref, gw, skip,
    mixed, sums, squares, numer, scores,
):
    k = pl.program_id(0)

    @pl.when(lax.rem(k, PAIRS_PER_GROUP) == 0)
    def _():
        scores[...] = dot(cc[...], bc[...], 1, 1)

    @pl.when(k == 0)
    def _():
        squares[...] = jnp.zeros(squares.shape, f32)
        numer[...] = jnp.zeros(numer.shape, f32)

    cols = cols_ref[0]
    rowvals = rows_ref[0]
    x = xc[...]
    parts = []
    for j in range(2):
        m = scores[...] * fade(cols, rowvals, seg_ref[...], j) * rowvals[2 + j : 3 + j, :]
        parts.append(dot(m.astype(bf16), x[:, j * HEAD_DIM : (j + 1) * HEAD_DIM], 1, 0))
    within = jnp.concatenate(parts, axis=1)
    carried = dot(cc[...], state[...], 1, 1) * spread(cols, 2)
    m = within + carried + skip[...] * x.astype(f32)
    mixed[...] = m
    zz = z[...].astype(f32)
    gated = m * (zz * sigmoid(zz))
    squares[...] += gated * gated
    numer[...] += gated * gw[...]

    @pl.when(k == pl.num_programs(0) - 1)
    def _():
        sums[...] = pair_put(
            jnp.sum(squares[...], axis=1, keepdims=True),
            jnp.sum(numer[...], axis=1, keepdims=True),
        )


def back_kernel(
    xc, bc, cc, z, state, cols_ref, rows_ref, seg_ref, gw, skip, mixed, vcols,
    dz, dx, dcg, dbg, ds, colout, rowout, scores, dscores, dcacc,
):
    k = pl.program_id(0)
    place = lax.rem(k, PAIRS_PER_GROUP)

    @pl.when(place == 0)
    def _():
        scores[...] = dot(cc[...], bc[...], 1, 1)
        dscores[...] = jnp.zeros(dscores.shape, f32)
        dcacc[...] = jnp.zeros(dcacc.shape, f32)

    cols = cols_ref[0]
    rowvals = rows_ref[0]
    x = xc[...]
    zz = z[...].astype(f32)
    m = mixed[...]
    s = sigmoid(zz)
    gate = zz * s
    gated = m * gate
    dgated = vcols[:, 0:1] * (gw[...] - vcols[:, 1:2] * gated)
    dz[...] = (dgated * m * (s * (1.0 + zz * (1.0 - s)))).astype(bf16)
    dy = dgated * gate
    dyb = dy.astype(bf16)
    dyb_t = dy.T.astype(bf16)
    outs = []
    rowsums = []
    colsums = []
    for j in range(2):
        sl = slice(j * HEAD_DIM, (j + 1) * HEAD_DIM)
        dt_row = rowvals[2 + j : 3 + j, :]
        f = fade(cols, rowvals, seg_ref[...], j)
        fd = f * dt_row
        sc = scores[...]
        dm = dot(dyb[:, sl], x[:, sl], 1, 1)
        outs.append(dot(dyb_t[sl], (sc * fd).astype(bf16), 1, 0))
        dscores[...] += fd * dm
        q = sc * f * dm
        rowsums.append(jnp.sum(q * dt_row, axis=1, keepdims=True))
        colsums.append(jnp.sum(q, axis=0, keepdims=True))
    dx[...] = jnp.concatenate(outs, axis=0).T + skip[...] * dy
    reach = dy * spread(cols, 2)
    reachb = reach.astype(bf16)
    carried = dot(cc[...], state[...], 1, 1)
    both = reach * carried
    for j in range(2):
        sl = slice(j * HEAD_DIM, (j + 1) * HEAD_DIM)
        rowsums[j] = rowsums[j] + jnp.sum(both[:, sl], axis=1, keepdims=True)
    dcacc[...] += dot(reachb, state[...], 1, 0)
    ds[...] = dot(reachb, cc[...], 0, 0).astype(bf16)
    colout[0] = pair_put(*rowsums)
    sub = lax.broadcasted_iota(jnp.int32, (8, colsums[0].shape[1]), 0)
    rowout[0] = jnp.where(sub == 0, colsums[0], jnp.where(sub == 1, colsums[1], 0.0))

    @pl.when(place == PAIRS_PER_GROUP - 1)
    def _():
        d = dscores[...].astype(bf16)
        dcg[...] = dcacc[...] + dot(d, bc[...], 1, 0)
        dbg[...] = dot(d, cc[...], 0, 0)


def last_kernel(
    xc, bc, gstate, state, cols_ref, dx, dcg, dbg, ux, ub, uc, wx, wb, wc, valid_ref,
    gx, gb, gc, hx, hb, hc, lx, lb, lc, stats, inner, dbacc, ext,
):
    k = pl.program_id(0)
    place = lax.rem(k, PAIRS_PER_GROUP)
    valid = valid_ref[...]
    rows = xc.shape[0]

    def finish(grad, u, w, out, head, last):
        g, h = conv_back(ext, silu_back(grad, u[...]), w, valid)
        out[...] = g.astype(bf16)
        head[...] = h
        last[...] = g[rows - 8 :, :]

    @pl.when(place == 0)
    def _():
        dbacc[...] = dbg[...]
        finish(dcg[...], uc, wc, gc, hc, lc)

    cols = cols_ref[0]
    x = xc[...].astype(f32)
    we = spread(cols, 4)
    g = gstate[...]
    gbx = dot(bc[...], g, 1, 1)
    xg = x * gbx
    stats[0] = pair_put(
        jnp.sum(xg[:, :HEAD_DIM], axis=1, keepdims=True),
        jnp.sum(xg[:, HEAD_DIM:], axis=1, keepdims=True),
    )
    gs = g.astype(f32) * state[...].astype(f32)
    sub = lax.broadcasted_iota(jnp.int32, (8, STATE), 0)
    inner[...] = jnp.where(
        sub == 0,
        jnp.sum(gs[:HEAD_DIM], axis=0, keepdims=True),
        jnp.where(sub == 1, jnp.sum(gs[HEAD_DIM:], axis=0, keepdims=True), 0.0),
    )[None]
    dbacc[...] += dot((x * we).astype(bf16), g, 1, 0)
    finish(dx[...] + we * gbx, ux, wx, gx, hx, lx)

    @pl.when(place == PAIRS_PER_GROUP - 1)
    def _():
        finish(dbacc[...], ub, wb, gb, hb, lb)


def shift_rows(values, amount):
    filler = jnp.zeros((amount,) + values.shape[1:], values.dtype)
    return jnp.concatenate([filler, values[: values.shape[0] - amount]], axis=0)


def hop(value, steps):
    count = lax.axis_size("ctx")
    initial, last = max(0, -steps), min(count, count - steps)
    return lax.ppermute(value, "ctx", [(i, i + steps) for i in range(initial, last)])


MESH = pl.DeviceIdType.MESH
CHUNKS = 8


def carry_kernel(sign, count, s_ref, mine_ref, peer_ref, out, other, came, going, sems):
    me = lax.axis_index("ctx")
    half = lax.rem(me, 2)
    pair = lax.div(me, 2)
    pairs = count // 2
    peer = me + 1 - 2 * half
    is_first = half == (0 if sign > 0 else 1)
    has_prev = (pair > 0) if sign > 0 else (pair < pairs - 1)
    has_next = (pair < pairs - 1) if sign > 0 else (pair > 0)
    heads = s_ref.shape[0]
    step = heads // CHUNKS

    barrier = pltpu.get_barrier_semaphore()
    pl.semaphore_signal(barrier, inc=1, device_id={"ctx": peer}, device_id_type=MESH)

    @pl.when(has_prev)
    def _():
        pl.semaphore_signal(barrier, inc=1, device_id={"ctx": me - 2 * sign}, device_id_type=MESH)

    @pl.when(has_next)
    def _():
        pl.semaphore_signal(barrier, inc=1, device_id={"ctx": me + 2 * sign}, device_id_type=MESH)

    pl.semaphore_wait(barrier, 1 + jnp.where(has_prev, 1, 0) + jnp.where(has_next, 1, 0))

    def swap(i):
        part = pl.ds(i * step, step)
        return pltpu.make_async_remote_copy(
            src_ref=s_ref.at[part], dst_ref=other.at[part], send_sem=sems.at[0, i],
            recv_sem=sems.at[1, i], device_id={"ctx": peer}, device_id_type=MESH,
        )

    def chain(i):
        part = pl.ds(i * step, step)
        return pltpu.make_async_remote_copy(
            src_ref=going.at[part], dst_ref=came.at[part], send_sem=sems.at[2, i],
            recv_sem=sems.at[3, i], device_id={"ctx": me + 2 * sign}, device_id_type=MESH,
        )

    for i in range(CHUNKS):
        swap(i).start()

    @pl.when(jnp.logical_not(has_prev))
    def _():
        came[...] = jnp.zeros(came.shape, bf16)

    for i in range(CHUNKS):
        part = slice(i * step, (i + 1) * step)
        swap(i).wait_recv()

        @pl.when(has_prev)
        def _():
            chain(i).wait_recv()

        base = came[part].astype(f32)
        own, got = s_ref[part].astype(f32), other[part].astype(f32)
        d_own, d_got = mine_ref[part], peer_ref[part]

        @pl.when(is_first)
        def _():
            out[part] = came[part]
            going[part] = (d_got * (d_own * base + own) + got).astype(bf16)

        @pl.when(jnp.logical_not(is_first))
        def _():
            mid = d_got * base + got
            out[part] = mid.astype(bf16)
            going[part] = (d_own * mid + own).astype(bf16)

        @pl.when(has_next)
        def _():
            chain(i).start()

    for i in range(CHUNKS):
        swap(i).wait_send()

        @pl.when(has_next)
        def _():
            chain(i).wait_send()


def carry(states, mine_decay, peer_decay, sign):
    count = lax.axis_size("ctx")
    heads = states.shape[0] // HEAD_DIM
    shape = (heads, HEAD_DIM, STATE)
    vmem = pl.BlockSpec(memory_space=pltpu.VMEM)
    out = pl.pallas_call(
        partial(carry_kernel, sign, count),
        out_shape=jax.ShapeDtypeStruct(shape, bf16),
        in_specs=[vmem] * 3,
        out_specs=vmem,
        scratch_shapes=[
            pltpu.VMEM(shape, bf16), pltpu.VMEM(shape, bf16), pltpu.VMEM(shape, bf16),
            pltpu.SemaphoreType.DMA((4, CHUNKS)),
        ],
        compiler_params=pltpu.CompilerParams(
            collective_id=0 if sign > 0 else 1, has_side_effects=True,
            vmem_limit_bytes=32 * 1024 * 1024,
        ),
    )(states.reshape(shape), mine_decay, peer_decay)
    return out.reshape(states.shape)


def swap_barrier(peer):
    barrier = pltpu.get_barrier_semaphore()
    pl.semaphore_signal(barrier, inc=1, device_id={"tp": peer}, device_id_type=MESH)
    pl.semaphore_wait(barrier, 1)


def move_kernel(to_heads, count, *refs):
    ins, outs, sems = refs[:count], refs[count : 2 * count], refs[2 * count]
    me = lax.axis_index("tp")
    peer = 1 - me
    swap_barrier(peer)
    copies = []
    for i in range(count):
        a, o = ins[i], outs[i]
        if to_heads:
            rows, width = a.shape[0], o.shape[1]
            there = pl.ds(pl.multiple_of(peer * width, 128), width)
            here = pl.ds(pl.multiple_of(me * width, 128), width)
            place = pl.ds(pl.multiple_of(me * rows, 8), rows)
            send, keep, dst = a.at[:, there], a.at[:, here], o.at[place, :]
        else:
            rows, width = o.shape[0], a.shape[1]
            there = pl.ds(pl.multiple_of(peer * rows, 8), rows)
            here = pl.ds(pl.multiple_of(me * rows, 8), rows)
            place = pl.ds(pl.multiple_of(me * width, 128), width)
            send, keep, dst = a.at[there, :], a.at[here, :], o.at[:, place]
        away = pltpu.make_async_remote_copy(
            src_ref=send, dst_ref=dst, send_sem=sems.at[0, i], recv_sem=sems.at[1, i],
            device_id={"tp": peer}, device_id_type=MESH,
        )
        away.start()
        local = pltpu.make_async_copy(keep, dst, sems.at[2, i])
        local.start()
        copies.append((away, local))
    for away, local in copies:
        away.wait()
        local.wait()


def move(arrays, to_heads, collective):
    count = len(arrays)
    anywhere = pl.BlockSpec(memory_space=pltpu.VMEM)
    shapes = []
    for a in arrays:
        r, w = a.shape
        shapes.append(jax.ShapeDtypeStruct((2 * r, w // 2) if to_heads else (r // 2, 2 * w), a.dtype))
    return pl.pallas_call(
        partial(move_kernel, to_heads, count),
        out_shape=shapes,
        in_specs=[anywhere] * count,
        out_specs=[anywhere] * count,
        scratch_shapes=[pltpu.SemaphoreType.DMA((3, count))],
        compiler_params=pltpu.CompilerParams(
            collective_id=collective, has_side_effects=True, vmem_limit_bytes=32 * 1024 * 1024
        ),
    )(*arrays)


def shards(
    x_in, b_in, c_in, z_in, dt_raw, conv_x, conv_b, conv_c, decay_rate, dt_bias, skip_scale,
    norm_gain, w_value, resets, bucket, return_table,
):
    tok = x_in.shape[0]
    tp = lax.axis_index("tp")
    tpn = lax.axis_size("tp")

    part_heads = dt_raw.shape[1] // tpn
    lanes = ((0, 0), (0, 128 - part_heads))
    dt_wide = jnp.concatenate(
        [jnp.pad(dt_raw[:, :part_heads], lanes), jnp.pad(dt_raw[:, part_heads:], lanes)], axis=1
    )
    x, b, c, z, dt_got = move([x_in, b_in, c_in, z_in, dt_wide], True, 2)
    dt_in = dt_got[:, :part_heads].astype(f32)
    T = x.shape[0]
    W, N, H = x.shape[1], b.shape[1], dt_in.shape[1]
    pairs = H // 2

    def mine(a, width):
        return lax.dynamic_slice_in_dim(a, tp * width, width, a.ndim - 1)

    wx, wb, wc = mine(conv_x, W), mine(conv_b, N), mine(conv_c, N)
    rate, bias, skip = mine(decay_rate, H), mine(dt_bias, H), mine(skip_scale, H)
    gw = mine(norm_gain * w_value, W)[None, :]
    skip_row = jnp.repeat(skip, HEAD_DIM)[None, :]

    real = resets.astype(f32)
    keep = jnp.stack([1.0 - jnp.maximum(real[-2], real[-1]), 1.0 - real[-1], jnp.ones((), f32)])
    second = jnp.maximum(real, shift_rows(real, 1))
    third = jnp.maximum(second, shift_rows(real, 2))
    valid = 1.0 - jnp.stack([real, second, third] + [real] * 5, axis=1)

    outgoing = jnp.concatenate([x[-3:], b[-3:], c[-3:]], axis=1) * keep.astype(bf16)[:, None]
    incoming = jnp.pad(hop(outgoing, 1).astype(f32), ((5, 0), (0, 0)))
    tx, tb, tc = incoming[:, :W], incoming[:, W : W + N], incoming[:, W + N :]

    dt_pre = dt_in + bias[None, :]
    dt = jax.nn.softplus(dt_pre)
    r_i = lax.broadcasted_iota(jnp.int32, (T, T), 0)
    c_i = lax.broadcasted_iota(jnp.int32, (T, T), 1)
    lower = jnp.where(r_i >= c_i, 1.0, 0.0)
    sums = jnp.dot(
        lower, jnp.concatenate([-dt * rate[None, :], real[:, None]], axis=1), precision=highest
    )
    cum, counts = sums[:, :H], jnp.round(sums[:, H])
    seg = jnp.where((r_i >= c_i) & (counts[:, None] == counts[None, :]), 0.0, -1e30)
    reach = jnp.exp(cum) * jnp.where(counts == 0.0, 1.0, 0.0)[:, None]
    tail_decay = jnp.exp(cum[-1][None, :] - cum) * jnp.where(counts == counts[-1], 1.0, 0.0)[:, None]
    we = tail_decay * dt
    decay = reach[-1]
    count = lax.axis_size("ctx")
    peer = lax.ppermute(decay, "ctx", [(i, i ^ 1) for i in range(count)])
    mine_decay = jnp.broadcast_to(decay[:, None, None], (H, 1, STATE))
    peer_decay = jnp.broadcast_to(peer[:, None, None], (H, 1, STATE))

    def to_pairs(a):
        return a.reshape(T, pairs, 2).transpose(1, 0, 2)

    cols = jnp.concatenate([to_pairs(cum), to_pairs(reach), to_pairs(we), to_pairs(tail_decay)], 2)
    rowvals = jnp.concatenate(
        [cum.T.reshape(pairs, 2, T), dt.T.reshape(pairs, 2, T), jnp.zeros((pairs, 4, T), f32)], 1
    )

    def sds(shape, dtype=f32):
        return jax.ShapeDtypeStruct(shape, dtype)

    per = PAIRS_PER_GROUP
    px = pl.BlockSpec((T, PAIR), lambda k: (0, k))
    pg = pl.BlockSpec((T, STATE), lambda k: (0, k // per))
    t8x = pl.BlockSpec((8, PAIR), lambda k: (0, k))
    t8g = pl.BlockSpec((8, STATE), lambda k: (0, k // per))
    w4x = pl.BlockSpec((4, PAIR), lambda k: (0, k))
    w4g = pl.BlockSpec((4, STATE), lambda k: (0, k // per))
    r1x = pl.BlockSpec((1, PAIR), lambda k: (0, k))
    v8 = pl.BlockSpec((T, 8), lambda k: (0, 0))
    c8 = pl.BlockSpec((1, T, 8), lambda k: (k, 0, 0))
    r8 = pl.BlockSpec((1, 8, T), lambda k: (k, 0, 0))
    st = pl.BlockSpec((PAIR, STATE), lambda k: (k, 0))
    tt = pl.BlockSpec((T, T), lambda k: (0, 0))
    params = pltpu.CompilerParams(
        dimension_semantics=("arbitrary",), vmem_limit_bytes=32 * 1024 * 1024
    )
    ext = pltpu.VMEM((T + 16, PAIR), f32)
    square = pltpu.VMEM((T, T), f32)

    xc, bc, cc, ux, ub, uc, add = pl.pallas_call(
        conv_kernel,
        grid=(pairs,),
        in_specs=[px, pg, pg, t8x, t8g, t8g, w4x, w4g, w4g, v8, c8],
        out_specs=[px, pg, pg, px, pg, pg, st],
        out_shape=[
            sds((T, W), bf16), sds((T, N), bf16), sds((T, N), bf16),
            sds((T, W)), sds((T, N)), sds((T, N)), sds((W, STATE), bf16),
        ],
        scratch_shapes=[ext],
        compiler_params=params,
    )(x, b, c, tx, tb, tc, wx, wb, wc, valid, cols)

    state = carry(add, mine_decay, peer_decay, 1)

    mixed, sums_out = pl.pallas_call(
        mix_kernel,
        grid=(pairs,),
        in_specs=[px, pg, pg, px, st, c8, r8, tt, r1x, r1x],
        out_specs=[px, v8],
        out_shape=[sds((T, W)), sds((T, 8))],
        scratch_shapes=[pltpu.VMEM((T, PAIR), f32), pltpu.VMEM((T, PAIR), f32), square],
        compiler_params=params,
    )(xc, bc, cc, z, state, cols, rowvals, seg, gw, skip_row)

    both = lax.psum(sums_out[:, :2].T, "tp")
    width_all = W * tpn
    rms = jnp.sqrt(both[0] / width_all + epsilon)
    values = both[1] / rms
    table_n = return_table.shape[0]
    onehot = bucket[:, None] == lax.broadcasted_iota(jnp.int32, (1, table_n), 1)
    target = jnp.sum(jnp.where(onehot, return_table[None, :], 0.0), axis=1)
    vscale = (values - target) / rms
    vcols = jnp.stack([vscale, values / (rms * width_all)] + [vscale] * 6, axis=1)

    dz, dx, dcg, dbg, ds, colout, rowout = pl.pallas_call(
        back_kernel,
        grid=(pairs,),
        in_specs=[px, pg, pg, px, st, c8, r8, tt, r1x, r1x, px, v8],
        out_specs=[px, px, pg, pg, st, c8, r8],
        out_shape=[
            sds((T, W), bf16), sds((T, W)), sds((T, N)), sds((T, N)), sds((W, STATE), bf16),
            sds((pairs, T, 8)), sds((pairs, 8, T)),
        ],
        scratch_shapes=[square, square, pltpu.VMEM((T, STATE), f32)],
        compiler_params=params,
    )(xc, bc, cc, z, state, cols, rowvals, seg, gw, skip_row, mixed, vcols)

    gstate = carry(ds, mine_decay, peer_decay, -1)

    gx, gb, gc, hx, hb, hc, lx, lb, lc, stats, inner = pl.pallas_call(
        last_kernel,
        grid=(pairs,),
        in_specs=[px, pg, st, st, c8, px, pg, pg, px, pg, pg, w4x, w4g, w4g, v8],
        out_specs=[px, pg, pg, t8x, t8g, t8g, t8x, t8g, t8g, c8, r8s(STATE)],
        out_shape=[
            sds((T, W), bf16), sds((T, N), bf16), sds((T, N), bf16),
            sds((8, W)), sds((8, N)), sds((8, N)), sds((8, W)), sds((8, N)), sds((8, N)),
            sds((pairs, T, 8)), sds((pairs, 8, STATE)),
        ],
        scratch_shapes=[pltpu.VMEM((T, STATE), f32), ext],
        compiler_params=params,
    )(xc, bc, gstate, state, cols, dx, dcg, dbg, ux, ub, uc, wx, wb, wc, valid)

    def from_cols(a):
        return a[:, :, :2].transpose(1, 0, 2).reshape(T, H)

    row_part = from_cols(colout)
    col_sum = rowout[:, :2, :].reshape(H, T).T
    xg = from_cols(stats)
    ginner = jnp.sum(inner[:, :2, :], axis=2).reshape(H)
    tail_part = we * xg
    dcum = row_part - dt * col_sum - tail_part
    at_end = jnp.sum(tail_part, axis=0) + decay * ginner
    rev_sum = jnp.dot(lower.T, dcum, precision=highest) + at_end[None, :]
    ddt = col_sum + tail_decay * xg - rate[None, :] * rev_sum
    ddt_wide = jnp.pad((ddt * jax.nn.sigmoid(dt_pre)).astype(bf16), lanes)

    heads3 = jnp.concatenate([hx, hb, hc], axis=1)[5:8]
    last3 = jnp.concatenate([lx, lb, lc], axis=1)[5:8]
    fixed = (last3 + hop(heads3, -1) * keep[:, None]).astype(bf16)
    gx = lax.dynamic_update_slice(gx, fixed[:, :W], (T - 3, 0))
    gb = lax.dynamic_update_slice(gb, fixed[:, W : W + N], (T - 3, 0))
    gc = lax.dynamic_update_slice(gc, fixed[:, W + N :], (T - 3, 0))
    out_values = lax.dynamic_slice_in_dim(values, tp * tok, tok, 0)
    grad_x, grad_b, grad_c, grad_z, dt_out = move([gx, gb, gc, dz, ddt_wide], False, 3)
    grad_dt = jnp.concatenate([dt_out[:, :part_heads], dt_out[:, 128 : 128 + part_heads]], axis=1)
    return (out_values, grad_x, grad_b, grad_c, grad_z, grad_dt)


def r8s(width):
    return pl.BlockSpec((1, 8, width), lambda k: (k, 0, 0))


def solution(mesh):
    row = P(("group", "ctx", "tp"), None)
    seq = P(("group", "ctx"))
    return jax.shard_map(
        shards,
        mesh=mesh,
        in_specs=(row,) * 5 + (P(),) * 8 + (seq, seq, P()),
        out_specs=(P(("group", "ctx", "tp")),) + (row,) * 5,
        check_vma=False,
    )
```

```python
from functools import partial

import jax
import jax.numpy as jnp
from jax import lax
from jax.experimental import pallas as pl
from jax.experimental.pallas import tpu as pltpu
from jax.sharding import PartitionSpec as P

HEADS = 64
HEAD_DIM = 64
GROUPS = 4
STATE = 128
PAIR = 2 * HEAD_DIM
PAIRS_PER_GROUP = HEADS // GROUPS // 2

epsilon = 1e-05
highest = lax.Precision.HIGHEST
f32 = jnp.float32
bf16 = jnp.bfloat16


def dot(a, b, ca, cb):
    return lax.dot_general(a, b, (((ca,), (cb,)), ((), ())), preferred_element_type=f32)


def sigmoid(u):
    return 1.0 / (1.0 + jnp.exp(-u))


def conv_pre(ext, x_ref, tail_ref, w_ref, valid):
    rows = x_ref.shape[0]
    ext[0:8, :] = tail_ref[...]
    ext[8 : 8 + rows, :] = x_ref[...].astype(f32)
    total = w_ref[0:1, :] * ext[8 : 8 + rows, :]
    for k in range(1, 4):
        total = total + w_ref[k : k + 1, :] * ext[8 - k : 8 - k + rows, :] * valid[:, k - 1 : k]
    return total


def conv_back(ext, du, w_ref, valid):
    rows = du.shape[0]
    ext[...] = jnp.zeros(ext.shape, f32)
    grad = w_ref[0:1, :] * du
    head = jnp.zeros((8, du.shape[1]), f32)
    for k in range(1, 4):
        ext[8 : 8 + rows, :] = w_ref[k : k + 1, :] * du * valid[:, k - 1 : k]
        grad = grad + ext[8 + k : 8 + k + rows, :]
        head = head + ext[k : k + 8, :]
    return grad, head


def silu_back(grad, u):
    s = sigmoid(u)
    return grad * (s * (1.0 + u * (1.0 - s)))


def spread(cols, i):
    rows = cols.shape[0]
    lane = lax.broadcasted_iota(jnp.int32, (rows, PAIR), 1)
    return jnp.where(lane < HEAD_DIM, cols[:, i : i + 1], cols[:, i + 1 : i + 2])


def pair_put(*cols):
    rows = cols[0].shape[0]
    lane = lax.broadcasted_iota(jnp.int32, (rows, 8), 1)
    out = jnp.zeros((rows, 8), f32)
    for i, c in enumerate(cols):
        out = jnp.where(lane == i, c, out)
    return out


def lane_put(out, k, a, b):
    lane = lax.broadcasted_iota(jnp.int32, out.shape, 1)
    kept = out[...]
    out[...] = jnp.where(lane == 2 * k, a, jnp.where(lane == 2 * k + 1, b, kept))


def conv_kernel(
    x, b, c, tx, tb, tc, wx, wb, wc, valid_ref, cols_ref,
    xc, bc, cc, ux, ub, uc, add, ext,
):
    k = pl.program_id(0)
    valid = valid_ref[...]

    @pl.when(lax.rem(k, PAIRS_PER_GROUP) == 0)
    def _():
        u = conv_pre(ext, b, tb, wb, valid)
        ub[...] = u
        bc[...] = (u * sigmoid(u)).astype(bf16)
        u = conv_pre(ext, c, tc, wc, valid)
        uc[...] = u
        cc[...] = (u * sigmoid(u)).astype(bf16)

    u = conv_pre(ext, x, tx, wx, valid)
    ux[...] = u
    narrow = (u * sigmoid(u)).astype(bf16)
    xc[...] = narrow
    cols = cols_ref[0]
    weighted = (narrow.astype(f32) * spread(cols, 4)).astype(bf16)
    add[...] = dot(weighted, bc[...], 0, 0).astype(bf16)


def fade(cols, rowvals, seg, j):
    gap = cols[:, j : j + 1] - rowvals[j : j + 1, :]
    return jnp.exp(jnp.minimum(gap, 0.0) + seg)


def mix_kernel(
    xc, bc, cc, z, state, cols_ref, rows_ref, seg_ref, gw, skip,
    mixed, sums, squares, numer, scores,
):
    k = pl.program_id(0)

    @pl.when(lax.rem(k, PAIRS_PER_GROUP) == 0)
    def _():
        scores[...] = dot(cc[...], bc[...], 1, 1)

    @pl.when(k == 0)
    def _():
        squares[...] = jnp.zeros(squares.shape, f32)
        numer[...] = jnp.zeros(numer.shape, f32)

    cols = cols_ref[0]
    rowvals = rows_ref[0]
    x = xc[...]
    parts = []
    for j in range(2):
        m = scores[...] * fade(cols, rowvals, seg_ref[...], j) * rowvals[2 + j : 3 + j, :]
        parts.append(dot(m.astype(bf16), x[:, j * HEAD_DIM : (j + 1) * HEAD_DIM], 1, 0))
    within = jnp.concatenate(parts, axis=1)
    carried = dot(cc[...], state[...], 1, 1) * spread(cols, 2)
    m = within + carried + skip[...] * x.astype(f32)
    mixed[...] = m
    zz = z[...].astype(f32)
    gated = m * (zz * sigmoid(zz))
    squares[...] += gated * gated
    numer[...] += gated * gw[...]

    @pl.when(k == pl.num_programs(0) - 1)
    def _():
        sums[...] = pair_put(
            jnp.sum(squares[...], axis=1, keepdims=True),
            jnp.sum(numer[...], axis=1, keepdims=True),
        )


def back_kernel(
    xc, bc, cc, z, state, cols_ref, rows_ref, seg_ref, gw, skip, mixed, vcols,
    dz, dx, dcg, dbg, ds, colout, rowout, scores, dscores, dcacc,
):
    k = pl.program_id(0)
    place = lax.rem(k, PAIRS_PER_GROUP)

    @pl.when(place == 0)
    def _():
        scores[...] = dot(cc[...], bc[...], 1, 1)
        dscores[...] = jnp.zeros(dscores.shape, f32)
        dcacc[...] = jnp.zeros(dcacc.shape, f32)

    cols = cols_ref[0]
    rowvals = rows_ref[0]
    x = xc[...]
    zz = z[...].astype(f32)
    m = mixed[...]
    s = sigmoid(zz)
    gate = zz * s
    gated = m * gate
    dgated = vcols[:, 0:1] * (gw[...] - vcols[:, 1:2] * gated)
    dz[...] = (dgated * m * (s * (1.0 + zz * (1.0 - s)))).astype(bf16)
    dy = dgated * gate
    dyb = dy.astype(bf16)
    dyb_t = dy.T.astype(bf16)
    outs = []
    rowsums = []
    colsums = []
    for j in range(2):
        sl = slice(j * HEAD_DIM, (j + 1) * HEAD_DIM)
        dt_row = rowvals[2 + j : 3 + j, :]
        f = fade(cols, rowvals, seg_ref[...], j)
        fd = f * dt_row
        sc = scores[...]
        dm = dot(dyb[:, sl], x[:, sl], 1, 1)
        outs.append(dot(dyb_t[sl], (sc * fd).astype(bf16), 1, 0))
        dscores[...] += fd * dm
        q = sc * f * dm
        rowsums.append(jnp.sum(q * dt_row, axis=1, keepdims=True))
        colsums.append(jnp.sum(q, axis=0, keepdims=True))
    dx[...] = jnp.concatenate(outs, axis=0).T + skip[...] * dy
    reach = dy * spread(cols, 2)
    reachb = reach.astype(bf16)
    carried = dot(cc[...], state[...], 1, 1)
    both = reach * carried
    for j in range(2):
        sl = slice(j * HEAD_DIM, (j + 1) * HEAD_DIM)
        rowsums[j] = rowsums[j] + jnp.sum(both[:, sl], axis=1, keepdims=True)
    dcacc[...] += dot(reachb, state[...], 1, 0)
    ds[...] = dot(reachb, cc[...], 0, 0).astype(bf16)

    @pl.when(k == 0)
    def _():
        colout[...] = jnp.zeros(colout.shape, f32)

    lane_put(colout, k, rowsums[0], rowsums[1])
    sub = lax.broadcasted_iota(jnp.int32, (8, colsums[0].shape[1]), 0)
    rowout[0] = jnp.where(sub == 0, colsums[0], jnp.where(sub == 1, colsums[1], 0.0))

    @pl.when(place == PAIRS_PER_GROUP - 1)
    def _():
        d = dscores[...].astype(bf16)
        dcg[...] = dcacc[...] + dot(d, bc[...], 1, 0)
        dbg[...] = dot(d, cc[...], 0, 0)


def last_kernel(
    xc, bc, gstate, state, cols_ref, dx, dcg, dbg, ux, ub, uc, wx, wb, wc, valid_ref,
    gx, gb, gc, hx, hb, hc, lx, lb, lc, stats, inner, dbacc, ext,
):
    k = pl.program_id(0)
    place = lax.rem(k, PAIRS_PER_GROUP)
    valid = valid_ref[...]
    rows = xc.shape[0]

    def finish(grad, u, w, out, head, last):
        g, h = conv_back(ext, silu_back(grad, u[...]), w, valid)
        out[...] = g.astype(bf16)
        head[...] = h
        last[...] = g[rows - 8 :, :]

    @pl.when(place == 0)
    def _():
        dbacc[...] = dbg[...]
        finish(dcg[...], uc, wc, gc, hc, lc)

    cols = cols_ref[0]
    x = xc[...].astype(f32)
    we = spread(cols, 4)
    g = gstate[...]
    gbx = dot(bc[...], g, 1, 1)
    xg = x * gbx

    @pl.when(k == 0)
    def _():
        stats[...] = jnp.zeros(stats.shape, f32)

    lane_put(
        stats, k,
        jnp.sum(xg[:, :HEAD_DIM], axis=1, keepdims=True),
        jnp.sum(xg[:, HEAD_DIM:], axis=1, keepdims=True),
    )
    gs = g.astype(f32) * state[...].astype(f32)
    sub = lax.broadcasted_iota(jnp.int32, (8, STATE), 0)
    inner[...] = jnp.where(
        sub == 0,
        jnp.sum(gs[:HEAD_DIM], axis=0, keepdims=True),
        jnp.where(sub == 1, jnp.sum(gs[HEAD_DIM:], axis=0, keepdims=True), 0.0),
    )[None]
    dbacc[...] += dot((x * we).astype(bf16), g, 1, 0)
    finish(dx[...] + we * gbx, ux, wx, gx, hx, lx)

    @pl.when(place == PAIRS_PER_GROUP - 1)
    def _():
        finish(dbacc[...], ub, wb, gb, hb, lb)


def shift_rows(values, amount):
    filler = jnp.zeros((amount,) + values.shape[1:], values.dtype)
    return jnp.concatenate([filler, values[: values.shape[0] - amount]], axis=0)


def hop(value, steps):
    count = lax.axis_size("ctx")
    initial, last = max(0, -steps), min(count, count - steps)
    return lax.ppermute(value, "ctx", [(i, i + steps) for i in range(initial, last)])


MESH = pl.DeviceIdType.MESH
CHUNKS = 8


def carry_kernel(sign, count, s_ref, mine_ref, peer_ref, out, other, came, going, sems):
    me = lax.axis_index("ctx")
    half = lax.rem(me, 2)
    pair = lax.div(me, 2)
    pairs = count // 2
    peer = me + 1 - 2 * half
    is_first = half == (0 if sign > 0 else 1)
    has_prev = (pair > 0) if sign > 0 else (pair < pairs - 1)
    has_next = (pair < pairs - 1) if sign > 0 else (pair > 0)
    heads = s_ref.shape[0]
    step = heads // CHUNKS

    barrier = pltpu.get_barrier_semaphore()
    pl.semaphore_signal(barrier, inc=1, device_id={"ctx": peer}, device_id_type=MESH)

    @pl.when(has_prev)
    def _():
        pl.semaphore_signal(barrier, inc=1, device_id={"ctx": me - 2 * sign}, device_id_type=MESH)

    @pl.when(has_next)
    def _():
        pl.semaphore_signal(barrier, inc=1, device_id={"ctx": me + 2 * sign}, device_id_type=MESH)

    pl.semaphore_wait(barrier, 1 + jnp.where(has_prev, 1, 0) + jnp.where(has_next, 1, 0))

    def swap(i):
        part = pl.ds(i * step, step)
        return pltpu.make_async_remote_copy(
            src_ref=s_ref.at[part], dst_ref=other.at[part], send_sem=sems.at[0, i],
            recv_sem=sems.at[1, i], device_id={"ctx": peer}, device_id_type=MESH,
        )

    def chain(i):
        part = pl.ds(i * step, step)
        return pltpu.make_async_remote_copy(
            src_ref=going.at[part], dst_ref=came.at[part], send_sem=sems.at[2, i],
            recv_sem=sems.at[3, i], device_id={"ctx": me + 2 * sign}, device_id_type=MESH,
        )

    for i in range(CHUNKS):
        swap(i).start()

    @pl.when(jnp.logical_not(has_prev))
    def _():
        came[...] = jnp.zeros(came.shape, bf16)

    for i in range(CHUNKS):
        part = slice(i * step, (i + 1) * step)
        swap(i).wait_recv()

        @pl.when(has_prev)
        def _():
            chain(i).wait_recv()

        base = came[part].astype(f32)
        own, got = s_ref[part].astype(f32), other[part].astype(f32)
        d_own, d_got = mine_ref[part], peer_ref[part]

        @pl.when(is_first)
        def _():
            out[part] = came[part]
            going[part] = (d_got * (d_own * base + own) + got).astype(bf16)

        @pl.when(jnp.logical_not(is_first))
        def _():
            mid = d_got * base + got
            out[part] = mid.astype(bf16)
            going[part] = (d_own * mid + own).astype(bf16)

        @pl.when(has_next)
        def _():
            chain(i).start()

    for i in range(CHUNKS):
        swap(i).wait_send()

        @pl.when(has_next)
        def _():
            chain(i).wait_send()


def carry(states, mine_decay, peer_decay, sign):
    count = lax.axis_size("ctx")
    heads = states.shape[0] // HEAD_DIM
    shape = (heads, HEAD_DIM, STATE)
    vmem = pl.BlockSpec(memory_space=pltpu.VMEM)
    out = pl.pallas_call(
        partial(carry_kernel, sign, count),
        out_shape=jax.ShapeDtypeStruct(shape, bf16),
        in_specs=[vmem] * 3,
        out_specs=vmem,
        scratch_shapes=[
            pltpu.VMEM(shape, bf16), pltpu.VMEM(shape, bf16), pltpu.VMEM(shape, bf16),
            pltpu.SemaphoreType.DMA((4, CHUNKS)),
        ],
        compiler_params=pltpu.CompilerParams(
            collective_id=0 if sign > 0 else 1, has_side_effects=True,
            vmem_limit_bytes=32 * 1024 * 1024,
        ),
    )(states.reshape(shape), mine_decay, peer_decay)
    return out.reshape(states.shape)


def swap_barrier(peer):
    barrier = pltpu.get_barrier_semaphore()
    pl.semaphore_signal(barrier, inc=1, device_id={"tp": peer}, device_id_type=MESH)
    pl.semaphore_wait(barrier, 1)


def move_kernel(to_heads, count, *refs):
    ins, outs, sems = refs[:count], refs[count : 2 * count], refs[2 * count]
    me = lax.axis_index("tp")
    peer = 1 - me
    swap_barrier(peer)
    copies = []
    for i in range(count):
        a, o = ins[i], outs[i]
        if to_heads:
            rows, width = a.shape[0], o.shape[1]
            there = pl.ds(pl.multiple_of(peer * width, 128), width)
            here = pl.ds(pl.multiple_of(me * width, 128), width)
            place = pl.ds(pl.multiple_of(me * rows, 8), rows)
            send, keep, dst = a.at[:, there], a.at[:, here], o.at[place, :]
        else:
            rows, width = o.shape[0], a.shape[1]
            there = pl.ds(pl.multiple_of(peer * rows, 8), rows)
            here = pl.ds(pl.multiple_of(me * rows, 8), rows)
            place = pl.ds(pl.multiple_of(me * width, 128), width)
            send, keep, dst = a.at[there, :], a.at[here, :], o.at[:, place]
        away = pltpu.make_async_remote_copy(
            src_ref=send, dst_ref=dst, send_sem=sems.at[0, i], recv_sem=sems.at[1, i],
            device_id={"tp": peer}, device_id_type=MESH,
        )
        away.start()
        local = pltpu.make_async_copy(keep, dst, sems.at[2, i])
        local.start()
        copies.append((away, local))
    for away, local in copies:
        away.wait()
        local.wait()


def move(arrays, to_heads, collective):
    count = len(arrays)
    anywhere = pl.BlockSpec(memory_space=pltpu.VMEM)
    shapes = []
    for a in arrays:
        r, w = a.shape
        shapes.append(jax.ShapeDtypeStruct((2 * r, w // 2) if to_heads else (r // 2, 2 * w), a.dtype))
    return pl.pallas_call(
        partial(move_kernel, to_heads, count),
        out_shape=shapes,
        in_specs=[anywhere] * count,
        out_specs=[anywhere] * count,
        scratch_shapes=[pltpu.SemaphoreType.DMA((3, count))],
        compiler_params=pltpu.CompilerParams(
            collective_id=collective, has_side_effects=True, vmem_limit_bytes=32 * 1024 * 1024
        ),
    )(*arrays)


def shards(
    x_in, b_in, c_in, z_in, dt_raw, conv_x, conv_b, conv_c, decay_rate, dt_bias, skip_scale,
    norm_gain, w_value, resets, bucket, return_table,
):
    tok = x_in.shape[0]
    tp = lax.axis_index("tp")
    tpn = lax.axis_size("tp")

    part_heads = dt_raw.shape[1] // tpn
    lanes = ((0, 0), (0, 128 - part_heads))
    dt_wide = jnp.concatenate(
        [jnp.pad(dt_raw[:, :part_heads], lanes), jnp.pad(dt_raw[:, part_heads:], lanes)], axis=1
    )
    x, b, c, z, dt_got = move([x_in, b_in, c_in, z_in, dt_wide], True, 2)
    dt_in = dt_got[:, :part_heads].astype(f32)
    T = x.shape[0]
    W, N, H = x.shape[1], b.shape[1], dt_in.shape[1]
    pairs = H // 2

    def mine(a, width):
        return lax.dynamic_slice_in_dim(a, tp * width, width, a.ndim - 1)

    wx, wb, wc = mine(conv_x, W), mine(conv_b, N), mine(conv_c, N)
    rate, bias, skip = mine(decay_rate, H), mine(dt_bias, H), mine(skip_scale, H)
    gw = mine(norm_gain * w_value, W)[None, :]
    skip_row = jnp.repeat(skip, HEAD_DIM)[None, :]

    real = resets.astype(f32)
    keep = jnp.stack([1.0 - jnp.maximum(real[-2], real[-1]), 1.0 - real[-1], jnp.ones((), f32)])
    second = jnp.maximum(real, shift_rows(real, 1))
    third = jnp.maximum(second, shift_rows(real, 2))
    valid = 1.0 - jnp.stack([real, second, third] + [real] * 5, axis=1)

    outgoing = jnp.concatenate([x[-3:], b[-3:], c[-3:]], axis=1) * keep.astype(bf16)[:, None]
    incoming = jnp.pad(hop(outgoing, 1).astype(f32), ((5, 0), (0, 0)))
    tx, tb, tc = incoming[:, :W], incoming[:, W : W + N], incoming[:, W + N :]

    dt_pre = dt_in + bias[None, :]
    dt = jax.nn.softplus(dt_pre)
    r_i = lax.broadcasted_iota(jnp.int32, (T, T), 0)
    c_i = lax.broadcasted_iota(jnp.int32, (T, T), 1)
    lower = jnp.where(r_i >= c_i, 1.0, 0.0)
    sums = jnp.dot(
        lower, jnp.concatenate([-dt * rate[None, :], real[:, None]], axis=1), precision=highest
    )
    cum, counts = sums[:, :H], jnp.round(sums[:, H])
    seg = jnp.where((r_i >= c_i) & (counts[:, None] == counts[None, :]), 0.0, -1e30)
    reach = jnp.exp(cum) * jnp.where(counts == 0.0, 1.0, 0.0)[:, None]
    tail_decay = jnp.exp(cum[-1][None, :] - cum) * jnp.where(counts == counts[-1], 1.0, 0.0)[:, None]
    we = tail_decay * dt
    decay = reach[-1]
    count = lax.axis_size("ctx")
    peer = lax.ppermute(decay, "ctx", [(i, i ^ 1) for i in range(count)])
    mine_decay = jnp.broadcast_to(decay[:, None, None], (H, 1, STATE))
    peer_decay = jnp.broadcast_to(peer[:, None, None], (H, 1, STATE))

    def to_pairs(a):
        return a.reshape(T, pairs, 2).transpose(1, 0, 2)

    cols = jnp.concatenate([to_pairs(cum), to_pairs(reach), to_pairs(we), to_pairs(tail_decay)], 2)
    rowvals = jnp.concatenate(
        [cum.T.reshape(pairs, 2, T), dt.T.reshape(pairs, 2, T), jnp.zeros((pairs, 4, T), f32)], 1
    )

    def sds(shape, dtype=f32):
        return jax.ShapeDtypeStruct(shape, dtype)

    per = PAIRS_PER_GROUP
    px = pl.BlockSpec((T, PAIR), lambda k: (0, k))
    pg = pl.BlockSpec((T, STATE), lambda k: (0, k // per))
    t8x = pl.BlockSpec((8, PAIR), lambda k: (0, k))
    t8g = pl.BlockSpec((8, STATE), lambda k: (0, k // per))
    w4x = pl.BlockSpec((4, PAIR), lambda k: (0, k))
    w4g = pl.BlockSpec((4, STATE), lambda k: (0, k // per))
    r1x = pl.BlockSpec((1, PAIR), lambda k: (0, k))
    v8 = pl.BlockSpec((T, 8), lambda k: (0, 0))
    c8 = pl.BlockSpec((1, T, 8), lambda k: (k, 0, 0))
    r8 = pl.BlockSpec((1, 8, T), lambda k: (k, 0, 0))
    st = pl.BlockSpec((PAIR, STATE), lambda k: (k, 0))
    tt = pl.BlockSpec((T, T), lambda k: (0, 0))
    lane_width = -(-H // 128) * 128
    wide = pl.BlockSpec((T, lane_width), lambda k: (0, 0))
    params = pltpu.CompilerParams(
        dimension_semantics=("arbitrary",), vmem_limit_bytes=32 * 1024 * 1024
    )
    ext = pltpu.VMEM((T + 16, PAIR), f32)
    square = pltpu.VMEM((T, T), f32)

    xc, bc, cc, ux, ub, uc, add = pl.pallas_call(
        conv_kernel,
        grid=(pairs,),
        in_specs=[px, pg, pg, t8x, t8g, t8g, w4x, w4g, w4g, v8, c8],
        out_specs=[px, pg, pg, px, pg, pg, st],
        out_shape=[
            sds((T, W), bf16), sds((T, N), bf16), sds((T, N), bf16),
            sds((T, W)), sds((T, N)), sds((T, N)), sds((W, STATE), bf16),
        ],
        scratch_shapes=[ext],
        compiler_params=params,
    )(x, b, c, tx, tb, tc, wx, wb, wc, valid, cols)

    state = carry(add, mine_decay, peer_decay, 1)

    mixed, sums_out = pl.pallas_call(
        mix_kernel,
        grid=(pairs,),
        in_specs=[px, pg, pg, px, st, c8, r8, tt, r1x, r1x],
        out_specs=[px, v8],
        out_shape=[sds((T, W)), sds((T, 8))],
        scratch_shapes=[pltpu.VMEM((T, PAIR), f32), pltpu.VMEM((T, PAIR), f32), square],
        compiler_params=params,
    )(xc, bc, cc, z, state, cols, rowvals, seg, gw, skip_row)

    both = lax.psum(sums_out[:, :2].T, "tp")
    width_all = W * tpn
    rms = jnp.sqrt(both[0] / width_all + epsilon)
    values = both[1] / rms
    table_n = return_table.shape[0]
    onehot = bucket[:, None] == lax.broadcasted_iota(jnp.int32, (1, table_n), 1)
    target = jnp.sum(jnp.where(onehot, return_table[None, :], 0.0), axis=1)
    vscale = (values - target) / rms
    vcols = jnp.stack([vscale, values / (rms * width_all)] + [vscale] * 6, axis=1)

    dz, dx, dcg, dbg, ds, colout, rowout = pl.pallas_call(
        back_kernel,
        grid=(pairs,),
        in_specs=[px, pg, pg, px, st, c8, r8, tt, r1x, r1x, px, v8],
        out_specs=[px, px, pg, pg, st, wide, r8],
        out_shape=[
            sds((T, W), bf16), sds((T, W)), sds((T, N)), sds((T, N)), sds((W, STATE), bf16),
            sds((T, lane_width)), sds((pairs, 8, T)),
        ],
        scratch_shapes=[square, square, pltpu.VMEM((T, STATE), f32)],
        compiler_params=params,
    )(xc, bc, cc, z, state, cols, rowvals, seg, gw, skip_row, mixed, vcols)

    gstate = carry(ds, mine_decay, peer_decay, -1)

    gx, gb, gc, hx, hb, hc, lx, lb, lc, stats, inner = pl.pallas_call(
        last_kernel,
        grid=(pairs,),
        in_specs=[px, pg, st, st, c8, px, pg, pg, px, pg, pg, w4x, w4g, w4g, v8],
        out_specs=[px, pg, pg, t8x, t8g, t8g, t8x, t8g, t8g, wide, r8s(STATE)],
        out_shape=[
            sds((T, W), bf16), sds((T, N), bf16), sds((T, N), bf16),
            sds((8, W)), sds((8, N)), sds((8, N)), sds((8, W)), sds((8, N)), sds((8, N)),
            sds((T, lane_width)), sds((pairs, 8, STATE)),
        ],
        scratch_shapes=[pltpu.VMEM((T, STATE), f32), ext],
        compiler_params=params,
    )(xc, bc, gstate, state, cols, dx, dcg, dbg, ux, ub, uc, wx, wb, wc, valid)

    row_part = colout[:, :H]
    col_sum = rowout[:, :2, :].reshape(H, T).T
    xg = stats[:, :H]
    ginner = jnp.sum(inner[:, :2, :], axis=2).reshape(H)
    tail_part = we * xg
    dcum = row_part - dt * col_sum - tail_part
    at_end = jnp.sum(tail_part, axis=0) + decay * ginner
    rev_sum = jnp.dot(lower.T, dcum, precision=highest) + at_end[None, :]
    ddt = col_sum + tail_decay * xg - rate[None, :] * rev_sum
    ddt_wide = jnp.pad((ddt * jax.nn.sigmoid(dt_pre)).astype(bf16), lanes)

    heads3 = jnp.concatenate([hx, hb, hc], axis=1)[5:8]
    last3 = jnp.concatenate([lx, lb, lc], axis=1)[5:8]
    fixed = (last3 + hop(heads3, -1) * keep[:, None]).astype(bf16)
    gx = lax.dynamic_update_slice(gx, fixed[:, :W], (T - 3, 0))
    gb = lax.dynamic_update_slice(gb, fixed[:, W : W + N], (T - 3, 0))
    gc = lax.dynamic_update_slice(gc, fixed[:, W + N :], (T - 3, 0))
    out_values = lax.dynamic_slice_in_dim(values, tp * tok, tok, 0)
    grad_x, grad_b, grad_c, grad_z, dt_out = move([gx, gb, gc, dz, ddt_wide], False, 3)
    grad_dt = jnp.concatenate([dt_out[:, :part_heads], dt_out[:, 128 : 128 + part_heads]], axis=1)
    return (out_values, grad_x, grad_b, grad_c, grad_z, grad_dt)


def r8s(width):
    return pl.BlockSpec((1, 8, width), lambda k: (k, 0, 0))


def solution(mesh):
    row = P(("group", "ctx", "tp"), None)
    seq = P(("group", "ctx"))
    return jax.shard_map(
        shards,
        mesh=mesh,
        in_specs=(row,) * 5 + (P(),) * 8 + (seq, seq, P()),
        out_specs=(P(("group", "ctx", "tp")),) + (row,) * 5,
        check_vma=False,
    )
```
